256 devices in a mesh: dp: 8 (over z), ctx: 32 (over x, y, core).
Axes of the slice: x: 4, y: 4, z: 8, core: 2. Of those that a mesh axis runs over, the one named last changes fastest.
Arguments:
- queries: bfloat16 [8, 4096, 4096], P('dp', 'ctx')
- keys: bfloat16 [8, 4096, 4096], P('dp', 'ctx')
- values: bfloat16 [8, 4096, 4096], P('dp', 'ctx'), may hold values from -6 to 6
- d_out: bfloat16 [8, 4096, 4096], P('dp', 'ctx'), may hold values from -6 to 6
- gains: float32 [2, 4096], P(None, 'dp'), may hold values from 0.5 to 2
- window_widths: int32 [32], P('ctx'), may hold values from 0 to 1
- global_blocks: int32 [8, 2], P('dp'), may hold values from 0 to 31, as said below
- random_blocks: int32 [8, 32, 3], P('dp'), may hold values from 0 to 31
Outputs:
- out: bfloat16 [8, 4096, 4096], P('dp', 'ctx')
- d_queries: bfloat16 [8, 4096, 4096], P('dp', 'ctx')
- d_keys: bfloat16 [8, 4096, 4096], P('dp', 'ctx')
- d_values: bfloat16 [8, 4096, 4096], P('dp', 'ctx')
- d_gains: float32 [2, 4096], P(None, 'dp')
The draws below stay inside these ranges and needn't reach their ends.
Inputs may be any that keep to these rules, and one draw needn't show every extreme that they name: `global_blocks`: the 2 ids of a sequence are different.
All inputs are finite; a program needn't handle non-finite values.
Results may differ from the reference program's by a relative error of at most 0.018.
The reference program's roundings to bfloat16 on the way (of `q_scaled`, `k_scaled`, `weights_b` and `d_scores`) count: a program that leaves them out, or rounds other values in their place, can miss the bound.
Values may be sent and summed in bfloat16 or wider, within the bound.
No kernel may reach another device: no remote copies, remote signals or barrier semaphores. Data moves between devices by JAX's collectives and lax.ppermute only.
A program may use at most 128 MiB of HBM per device.

```python
import math
import jax
import jax.numpy as jnp
from jax import lax

HEADS = 32
HD = 128
WMAX = 1
GLOB = 2
RAND = 3
SEQS = 8
SEQ_LEN = 4096
NB = 32
CHANNELS = 4096


def draw_queries(key, part):
    drawn = jax.random.normal(jax.random.fold_in(key, 1), (SEQS, SEQ_LEN, CHANNELS), jnp.float32)
    return drawn.astype(jnp.bfloat16)


def draw_keys(key, part):
    drawn = jax.random.normal(jax.random.fold_in(key, 2), (SEQS, SEQ_LEN, CHANNELS), jnp.float32)
    return drawn.astype(jnp.bfloat16)


def draw_global_blocks(key, part):
    seq_keys = jax.random.split(jax.random.fold_in(key, 5), SEQS)

    def pick_blocks(one_key):
        return jax.random.permutation(one_key, NB)[:GLOB].astype(jnp.int32)
    drawn = jax.vmap(pick_blocks)(seq_keys)
    lower = jax.random.permutation(jax.random.fold_in(key, 6), NB - 1)[:GLOB - 1].astype(jnp.int32)
    with_last = jnp.concatenate([jnp.full((1,), NB - 1, jnp.int32), lower])
    turn = jax.random.randint(jax.random.fold_in(key, 7), (), 0, GLOB)
    with_last = jnp.roll(with_last, turn)
    chosen = jax.random.randint(jax.random.fold_in(key, 8), (), 0, SEQS)
    rows = jnp.arange(SEQS)
    return jnp.where((rows == chosen)[:, None], with_last[None, :], drawn).astype(jnp.int32)


def place_ends(drawn, own_key, smallest, high):
    shape = drawn.shape
    place = [jax.random.randint(jax.random.fold_in(own_key, axis), (), 0, shape[axis]) for axis in range(len(shape))]
    drawn = drawn.at[tuple(place)].set(smallest)
    longest = shape.index(max(shape))
    place[longest] = (place[longest] + 1) % shape[longest]
    return drawn.at[tuple(place)].set(high)


def strengthened(drawn, key, source, target, blocks, factor):
    owner, partner = [(jnp.arange(drawn.shape[dim]) // (drawn.shape[dim] // blocks)).reshape([-1 if axis == dim else 1 for axis in range(drawn.ndim)]) for dim in (source, target)]
    chosen = jax.random.permutation(key, blocks)[partner]
    strong = (owner == chosen) | (owner == (partner + blocks // 2) % blocks)
    return jnp.where(strong, factor * drawn, drawn)


def level_of(stream_key, shape, cuts, least, top_value):
    gain, own = 1.0, jax.random.fold_in(stream_key, 6)
    for dim, blocks in cuts:
        heights = jnp.exp(jax.random.uniform(jax.random.fold_in(own, dim), (blocks,), jnp.float32, least / len(cuts), top_value / len(cuts)))
        gain = gain * jnp.repeat(heights, shape[dim] // blocks).reshape([-1 if axis == dim else 1 for axis in range(len(shape))])
    return gain


def noise(own_key, extent, deviation, bound, shards=(), kind=jnp.bfloat16):
    result = deviation * jax.random.normal(own_key, extent, jnp.float32)
    if shards:
        result = result * level_of(own_key, extent, shards, -0.22, 0.18)
    return jnp.clip(result, -bound, bound).astype(kind)


def gaussian_with(rng, dims, spread, limit, pieces, heavy, held_as=jnp.bfloat16):
    drawn = spread * jax.random.normal(rng, dims, jnp.float32)
    if pieces:
        drawn = drawn * level_of(rng, dims, pieces, -0.22, 0.18)
    return jnp.clip(strengthened(drawn, jax.random.fold_in(rng, 3), *heavy), -limit, limit).astype(held_as)


def setup_inputs(seed: int = 0) -> dict:
    arg_keys = jax.random.split(jax.random.key(seed), 9)
    return {
        "queries": draw_queries(jax.random.fold_in(arg_keys[8], 71), 0),
        "keys": draw_keys(jax.random.fold_in(arg_keys[8], 71), 0),
        "values": noise(arg_keys[2], (SEQS, SEQ_LEN, CHANNELS), 1.0, 6.0, ((0, 8), (1, 32))),
        "d_out": gaussian_with(arg_keys[3], (SEQS, SEQ_LEN, CHANNELS), 1.0, 6.0, ((0, 8), (1, 32)), (0, 2, 8, 2.0)),
        "gains": jnp.clip(jnp.exp(math.log(2.0) - 1.3862944 * jax.random.uniform(arg_keys[4], (2, CHANNELS), jnp.float32) ** level_of(arg_keys[4], (2, CHANNELS), ((1, 8),), -0.2, 0.2)), 0.5, 2.0),
        "window_widths": place_ends(jax.random.randint(arg_keys[5], (HEADS,), 0, WMAX + 1), jax.random.fold_in(arg_keys[5], 1), 0, WMAX).astype(jnp.int32),
        "global_blocks": draw_global_blocks(jax.random.fold_in(arg_keys[8], 71), 0),
        "random_blocks": place_ends(jax.random.randint(arg_keys[7], (SEQS, NB, RAND), 0, NB), jax.random.fold_in(arg_keys[7], 1), 0, NB - 1).astype(jnp.int32),
    }


NEG_FILL = -1e+30

def rounded(array_in):
    return lax.optimization_barrier(array_in.astype(jnp.bfloat16)).astype(jnp.float32)

def slot_table(global_ids, random_ids, widths):
    block_count = random_ids.shape[0]
    blocks = jnp.arange(block_count, dtype=jnp.int32)
    offsets = jnp.arange(-WMAX, WMAX + 1, dtype=jnp.int32)
    nearby = blocks[:, None] + offsets[None, :]
    inside = (nearby >= 0) & (nearby < block_count)
    in_window = jnp.abs(offsets)[None, :] <= widths[:, None]
    window_ok = inside[None, :, :] & in_window[:, None, :]
    global_cols = jnp.broadcast_to(global_ids.astype(jnp.int32)[None, :], (block_count, global_ids.shape[0]))
    slot_ids = jnp.concatenate([nearby, global_cols, random_ids.astype(jnp.int32)], axis=1)
    always_on = jnp.ones((widths.shape[0], block_count, global_ids.shape[0] + random_ids.shape[1]), dtype=jnp.bool_)
    listed = jnp.concatenate([window_ok, always_on], axis=2)
    slot_total = slot_ids.shape[1]
    matches = slot_ids[:, :, None] == slot_ids[:, None, :]
    position = jnp.arange(slot_total)
    earlier = position[None, :] < position[:, None]
    repeated = jnp.any(matches[None] & earlier[None, None] & listed[:, :, None, :], axis=3)
    usable = listed & jnp.logical_not(repeated)
    return (jnp.clip(slot_ids, 0, block_count - 1), usable)

def softmax_rows(scores):
    row_max = lax.optimization_barrier(jnp.max(scores, axis=-1, keepdims=True))
    exponent = jnp.exp(scores - row_max)
    return exponent / lax.optimization_barrier(jnp.sum(exponent, axis=-1, keepdims=True))

def attend(q_raw, k_raw, v_raw, d_raw, gain_q, gain_k, widths, global_ids, random_ids):
    length, head_count, head_dim = q_raw.shape
    block_count = random_ids.shape[0]
    block_len = length // block_count
    score_scale = 1.0 / math.sqrt(head_dim)
    slot_ids, usable = slot_table(global_ids, random_ids, widths)
    slot_total = slot_ids.shape[1]
    block_shape = (block_count, block_len, head_count, head_dim)
    q_scaled = rounded(q_raw.astype(jnp.float32) * gain_q)
    k_scaled = rounded(k_raw.astype(jnp.float32) * gain_k)
    v_float = v_raw.astype(jnp.float32)
    q_blocks = q_scaled.reshape(block_shape)
    k_blocks = k_scaled.reshape(block_shape)
    v_blocks = v_float.reshape(block_shape)
    k_slots = k_blocks[slot_ids].reshape(block_count, slot_total * block_len, head_count, head_dim)
    v_slots = v_blocks[slot_ids].reshape(block_count, slot_total * block_len, head_count, head_dim)
    allowed = jnp.repeat(jnp.transpose(usable, (1, 0, 2)), block_len, axis=2)
    scores = jnp.einsum('irhd,ijhd->ihrj', q_blocks, k_slots) * score_scale
    weights = softmax_rows(jnp.where(allowed[:, :, None, :], scores, NEG_FILL))
    weights_b = rounded(weights)
    attended = jnp.einsum('ihrj,ijhd->irhd', weights_b, v_slots)
    q_global = q_blocks[global_ids]
    full_w = softmax_rows(jnp.einsum('grhd,thd->ghrt', q_global, k_scaled) * score_scale)
    full_b = rounded(full_w)
    full_out = jnp.einsum('ghrt,thd->grhd', full_b, v_float)
    out_blocks = rounded(attended.at[global_ids].set(full_out))
    d_blocks = d_raw.astype(jnp.float32).reshape(block_shape)
    row_dot = lax.optimization_barrier(jnp.sum(d_blocks * out_blocks, axis=3))
    is_global = jnp.any(jnp.arange(block_count)[:, None] == global_ids[None, :], axis=1)
    d_rows = jnp.where(is_global[:, None, None, None], 0.0, d_blocks)
    dot_rows = jnp.where(is_global[:, None, None], 0.0, row_dot)
    d_weights = jnp.einsum('irhd,ijhd->ihrj', d_rows, v_slots)
    d_scores = rounded(weights * (d_weights - jnp.transpose(dot_rows, (0, 2, 1))[..., None]))
    dq_blocks = jnp.einsum('ihrj,ijhd->irhd', d_scores, k_slots) * score_scale
    dk_slots = (jnp.einsum('ihrj,irhd->ijhd', d_scores, q_blocks) * score_scale).reshape(block_count * slot_total, block_len, head_count, head_dim)
    dv_slots = jnp.einsum('ihrj,irhd->ijhd', weights_b, d_rows).reshape(block_count * slot_total, block_len, head_count, head_dim)
    flat_ids = slot_ids.reshape(-1)
    dk_blocks = jnp.zeros(block_shape, jnp.float32).at[flat_ids].add(dk_slots)
    dv_blocks = jnp.zeros(block_shape, jnp.float32).at[flat_ids].add(dv_slots)
    d_global = d_blocks[global_ids]
    d_full = jnp.einsum('grhd,thd->ghrt', d_global, v_float)
    full_scores = rounded(full_w * (d_full - jnp.transpose(row_dot[global_ids], (0, 2, 1))[..., None]))
    dq_blocks = dq_blocks.at[global_ids].add(jnp.einsum('ghrt,thd->grhd', full_scores, k_scaled) * score_scale)
    flat_shape = (length, head_count, head_dim)
    dq_all = dq_blocks.reshape(flat_shape)
    dk_all = dk_blocks.reshape(flat_shape) + jnp.einsum('ghrt,grhd->thd', full_scores, q_global) * score_scale
    dv_all = dv_blocks.reshape(flat_shape) + jnp.einsum('ghrt,grhd->thd', full_b, d_global)
    grad_q = (dq_all * gain_q).astype(jnp.bfloat16)
    grad_k = (dk_all * gain_k).astype(jnp.bfloat16)
    grad_v = dv_all.astype(jnp.bfloat16)
    gain_terms = jnp.stack([lax.optimization_barrier(jnp.sum(dq_all * q_raw.astype(jnp.float32), axis=0)), lax.optimization_barrier(jnp.sum(dk_all * k_raw.astype(jnp.float32), axis=0))])
    return (out_blocks.reshape(flat_shape).astype(jnp.bfloat16), grad_q, grad_k, grad_v, gain_terms)

def head_major(array_in):
    return jnp.transpose(array_in.reshape(SEQ_LEN, HEADS, HD), (1, 0, 2))

def token_major(array_in):
    return jnp.transpose(array_in[:, :, 0, :], (1, 0, 2)).reshape(SEQ_LEN, HEADS * HD)

def reference(queries, keys, values, d_out, gains, window_widths, global_blocks, random_blocks):
    gain_rows_q = gains[0].reshape(HEADS, HD)
    gain_rows_k = gains[1].reshape(HEADS, HD)

    def per_sequence(seq_items):
        q_seq, k_seq, v_seq, d_seq, global_ids, random_ids = seq_items

        def per_head(head_items):
            q_head, k_head, v_head, d_head, g_query, g_key, width_one = head_items
            return attend(q_head[:, None, :], k_head[:, None, :], v_head[:, None, :], d_head[:, None, :], g_query[None, :], g_key[None, :], width_one[None], global_ids, random_ids)
        results = lax.map(per_head, (head_major(q_seq), head_major(k_seq), head_major(v_seq), head_major(d_seq), gain_rows_q, gain_rows_k, window_widths))
        out_h, grad_q, grad_k, grad_v, terms = results
        return (token_major(out_h), token_major(grad_q), token_major(grad_k), token_major(grad_v), terms[:, :, 0, :])
    out, grad_q, grad_k, grad_v, terms = lax.map(per_sequence, (queries, keys, values, d_out, global_blocks, random_blocks))
    d_gains = jnp.transpose(lax.optimization_barrier(jnp.sum(terms, axis=0)), (1, 0, 2)).reshape(2, HEADS * HD)
    return (out, grad_q, grad_k, grad_v, d_gains)
```

```python
import functools
import math

import jax
import jax.numpy as jnp
from jax import lax
from jax.experimental import pallas as pl
from jax.experimental.pallas import tpu as pltpu
from jax.sharding import PartitionSpec as P

HD = 128
BLOCK = 128
SCALE = 1.0 / math.sqrt(HD)
SCALE_LOG2 = SCALE * math.log2(math.e)
PENALTY = 1e30
CHUNK = 4
F32 = jnp.float32
BF16 = jnp.bfloat16


def dot_nn(a, b):
    return lax.dot_general(a, b, (((1,), (0,)), ((), ())), preferred_element_type=F32)


def dot_nt(a, b):
    return lax.dot_general(a, b, (((1,), (1,)), ((), ())), preferred_element_type=F32)


def dot_tn(a, b):
    return lax.dot_general(a, b, (((0,), (0,)), ((), ())), preferred_element_type=F32)


def lane_fold(combine, wide):
    folded = wide[:, :128]
    for n in range(1, wide.shape[1] // 128):
        folded = combine(folded, wide[:, n * 128 : (n + 1) * 128])
    return folded


def attention_kernel(
    width_ref, global_ref, random_ref, x_ref, gain_ref, y_ref, terms_ref,
    ks_ref, p_ref, dk_ref, dv_ref, tq_ref,
):
    block_count = x_ref.shape[0]
    chunk_count = block_count // CHUNK
    gain_q = gain_ref[0:1, :]
    gain_k = gain_ref[1:2, :]
    g0 = global_ref[0, 0]
    g1 = global_ref[0, 1]
    wide = width_ref[0] >= 1
    low = jnp.minimum(g0, g1)
    high = jnp.maximum(g0, g1)

    def scale_keys(j, carry):
        ks_ref[j] = (x_ref[j, 1].astype(F32) * gain_k).astype(BF16)
        return carry

    lax.fori_loop(0, block_count, scale_keys, 0, unroll=4)

    q_raw = jnp.concatenate([x_ref[g0, 0], x_ref[g1, 0]], 0).astype(F32)
    q_scaled = (q_raw * gain_q).astype(BF16)
    d_out = jnp.concatenate([x_ref[g0, 3], x_ref[g1, 3]], 0)
    rows = 2 * BLOCK

    def key_chunk(c):
        return ks_ref[pl.ds(c * CHUNK, CHUNK)].reshape(CHUNK * BLOCK, HD)

    def value_chunk(c):
        return x_ref[pl.ds(c * CHUNK, CHUNK), 2].reshape(CHUNK * BLOCK, HD)

    def full_scores(c, top):
        scores = dot_nt(q_scaled, key_chunk(c))
        p_ref[c] = scores
        return jnp.maximum(top, lane_fold(jnp.maximum, scores))

    top = lax.fori_loop(0, chunk_count, full_scores, jnp.full((rows, 128), -3e38, F32))
    top = jnp.max(top, axis=1, keepdims=True) * SCALE_LOG2

    def full_exp(c, total):
        e = jnp.exp2(p_ref[c] * SCALE_LOG2 - top)
        p_ref[c] = e
        return total + lane_fold(jnp.add, e)

    total = lax.fori_loop(0, chunk_count, full_exp, jnp.zeros((rows, 128), F32))
    inverse = 1.0 / jnp.sum(total, axis=1, keepdims=True)

    def full_out(c, acc):
        p = p_ref[c] * inverse
        p_ref[c] = p
        p_b = p.astype(BF16)
        dv_t = dot_tn(d_out, p_b)
        for n in range(CHUNK):
            dv_ref[c * CHUNK + n] = dv_t[:, n * 128 : (n + 1) * 128]
        return acc + dot_nn(p_b, value_chunk(c))

    out = lax.fori_loop(0, chunk_count, full_out, jnp.zeros((rows, HD), F32)).astype(BF16)
    y_ref[g0, 0] = out[:BLOCK]
    y_ref[g1, 0] = out[BLOCK:]
    row_dot = jnp.sum(d_out.astype(F32) * out.astype(F32), axis=1, keepdims=True)

    def full_back(c, acc):
        dp = dot_nt(d_out, value_chunk(c))
        ds = (p_ref[c] * (dp - row_dot)).astype(BF16)
        dk_t = dot_tn(q_scaled, ds)
        for n in range(CHUNK):
            dk_ref[c * CHUNK + n] = dk_t[:, n * 128 : (n + 1) * 128]
        return acc + dot_nn(ds, key_chunk(c))

    dq = lax.fori_loop(0, chunk_count, full_back, jnp.zeros((rows, HD), F32)) * SCALE
    dq_b = (dq * gain_q).astype(BF16)
    y_ref[g0, 1] = dq_b[:BLOCK]
    y_ref[g1, 1] = dq_b[BLOCK:]
    terms = dq * q_raw
    tq_ref[...] = terms[:BLOCK] + terms[BLOCK:]

    def sparse_block(i):
        ids = [i]
        penalties = [jnp.float32(0.0)]
        candidates = [(i - 1, wide & (i > 0)), (i + 1, wide & (i < block_count - 1))]
        candidates += [(g0, None), (g1, None)]
        candidates += [(random_ref[0, i, n], None) for n in range(random_ref.shape[2])]
        for block_id, listed in candidates:
            unusable = functools.reduce(jnp.logical_or, [block_id == t for t in ids])
            if listed is not None:
                unusable = unusable | jnp.logical_not(listed)
            ids.append(jnp.where(unusable, i, block_id))
            penalties.append(jnp.where(unusable, jnp.float32(PENALTY), jnp.float32(0.0)))
        slots = len(ids)
        k_slots = jnp.concatenate([ks_ref[t] for t in ids], 0)
        v_slots = jnp.concatenate([x_ref[t, 2] for t in ids], 0)
        q_raw = x_ref[i, 0].astype(F32)
        q_scaled = (q_raw * gain_q).astype(BF16)
        d_out = x_ref[i, 3]
        scores = dot_nt(q_scaled, k_slots)
        dp = dot_nt(d_out, v_slots)
        top = jnp.max(lane_fold(jnp.maximum, scores), axis=1, keepdims=True) * SCALE_LOG2
        es = [
            jnp.exp2(scores[:, t * 128 : (t + 1) * 128] * SCALE_LOG2 - (top + penalties[t]))
            for t in range(slots)
        ]
        inverse = 1.0 / jnp.sum(functools.reduce(jnp.add, es), axis=1, keepdims=True)
        p = jnp.concatenate([e * inverse for e in es], 1)
        p_b = p.astype(BF16)
        out = dot_nn(p_b, v_slots).astype(BF16)
        y_ref[i, 0] = out
        row_dot = jnp.sum(d_out.astype(F32) * out.astype(F32), axis=1, keepdims=True)
        ds = (p * (dp - row_dot)).astype(BF16)
        dq = dot_nn(ds, k_slots) * SCALE
        y_ref[i, 1] = (dq * gain_q).astype(BF16)
        tq_ref[...] += dq * q_raw
        dv_t = dot_tn(d_out, p_b)
        dk_t = dot_tn(q_scaled, ds)
        for t in range(slots):
            dv_ref[ids[t]] += dv_t[:, t * 128 : (t + 1) * 128]
        for t in range(slots):
            dk_ref[ids[t]] += dk_t[:, t * 128 : (t + 1) * 128]

    def step(n, carry):
        i = n + (n >= low).astype(jnp.int32)
        i = i + (i >= high).astype(jnp.int32)
        sparse_block(i)
        return carry

    lax.fori_loop(0, block_count - 2, step, 0)

    def finish(j, acc):
        dk = dk_ref[j].T * SCALE
        y_ref[j, 2] = (dk * gain_k).astype(BF16)
        y_ref[j, 3] = dv_ref[j].T.astype(BF16)
        return acc + dk * x_ref[j, 1].astype(F32)

    tk = lax.fori_loop(0, block_count, finish, jnp.zeros((BLOCK, HD), F32))
    terms_ref[0:1, :] = jnp.sum(tq_ref[...], axis=0, keepdims=True)
    terms_ref[1:2, :] = jnp.sum(tk, axis=0, keepdims=True)


def attention(widths, global_ids, random_ids, x, gains):
    block_count = x.shape[0]
    smem = pl.BlockSpec(memory_space=pltpu.SMEM)
    vmem = pl.BlockSpec(memory_space=pltpu.VMEM)
    return pl.pallas_call(
        attention_kernel,
        out_shape=(
            jax.ShapeDtypeStruct((block_count, 4, BLOCK, HD), BF16),
            jax.ShapeDtypeStruct((2, HD), F32),
        ),
        in_specs=[smem, smem, smem, vmem, vmem],
        out_specs=(vmem, vmem),
        scratch_shapes=[
            pltpu.VMEM((block_count, BLOCK, HD), BF16),
            pltpu.VMEM((block_count // CHUNK, 2 * BLOCK, CHUNK * BLOCK), F32),
            pltpu.VMEM((block_count, HD, BLOCK), F32),
            pltpu.VMEM((block_count, HD, BLOCK), F32),
            pltpu.VMEM((BLOCK, HD), F32),
        ],
        compiler_params=pltpu.CompilerParams(vmem_limit_bytes=40 * 1024 * 1024),
        name="attention",
    )(widths, global_ids, random_ids, x, gains)


HEADS_A_STEP = 8


def split_kernel(q_ref, k_ref, v_ref, d_ref, x_ref):
    for n, ref in enumerate((q_ref, k_ref, v_ref, d_ref)):
        for h in range(HEADS_A_STEP):
            x_ref[h, n] = ref[0, :, h * HD : (h + 1) * HD]


def split_heads(arrays):
    _, tokens, channels = arrays[0].shape
    heads = channels // HD
    spec = pl.BlockSpec((1, tokens, HEADS_A_STEP * HD), lambda i: (0, 0, i))
    return pl.pallas_call(
        split_kernel,
        grid=(heads // HEADS_A_STEP,),
        out_shape=jax.ShapeDtypeStruct((heads, 4, tokens, HD), BF16),
        in_specs=[spec] * 4,
        out_specs=pl.BlockSpec((HEADS_A_STEP, 4, tokens, HD), lambda i: (i, 0, 0, 0)),
        compiler_params=pltpu.CompilerParams(vmem_limit_bytes=24 * 1024 * 1024),
        name="split_heads",
    )(*arrays)


def join_kernel(y_ref, o_ref, q_ref, k_ref, v_ref):
    for n, ref in enumerate((o_ref, q_ref, k_ref, v_ref)):
        for h in range(HEADS_A_STEP):
            ref[0, :, h * HD : (h + 1) * HD] = y_ref[h, n]


def join_heads(y):
    heads, _, tokens, _ = y.shape
    spec = pl.BlockSpec((1, tokens, HEADS_A_STEP * HD), lambda i: (0, 0, i))
    return pl.pallas_call(
        join_kernel,
        grid=(heads // HEADS_A_STEP,),
        out_shape=(jax.ShapeDtypeStruct((1, tokens, heads * HD), BF16),) * 4,
        in_specs=[pl.BlockSpec((HEADS_A_STEP, 4, tokens, HD), lambda i: (i, 0, 0, 0))],
        out_specs=(spec,) * 4,
        compiler_params=pltpu.CompilerParams(vmem_limit_bytes=24 * 1024 * 1024),
        name="join_heads",
    )(y)


def exchange(x):
    return lax.all_to_all(x, "ctx", split_axis=0, concat_axis=0, tiled=True)


def on_device(queries, keys, values, d_out, gains, window_widths, global_blocks, random_blocks):
    x = exchange(split_heads((queries, keys, values, d_out)))
    all_gains = lax.all_gather(gains, "dp", axis=1, tiled=True)
    own_gains = lax.dynamic_slice_in_dim(all_gains, lax.axis_index("ctx") * HD, HD, 1)
    y, terms = attention(window_widths, global_blocks, random_blocks, x, own_gains)
    out, d_queries, d_keys, d_values = join_heads(exchange(y))
    head_terms = lax.psum(terms, "dp")
    columns = lax.all_gather(head_terms, "ctx", axis=1, tiled=True)
    own_width = gains.shape[1]
    d_gains = lax.dynamic_slice_in_dim(columns, lax.axis_index("dp") * own_width, own_width, 1)
    return (out, d_queries, d_keys, d_values, d_gains)


def solution(mesh):
    tokens = P("dp", "ctx", None)
    return jax.shard_map(
        on_device,
        mesh=mesh,
        in_specs=(
            tokens, tokens, tokens, tokens,
            P(None, "dp"), P("ctx"), P("dp", None), P("dp", None, None),
        ),
        out_specs=(tokens, tokens, tokens, tokens, P(None, "dp")),
        check_vma=False,
    )
```

```python
import functools
import math

import jax
import jax.numpy as jnp
from jax import lax
from jax.experimental import pallas as pl
from jax.experimental.pallas import tpu as pltpu
from jax.sharding import PartitionSpec as P

HD = 128
BLOCK = 128
SCALE = 1.0 / math.sqrt(HD)
LOG2E = math.log2(math.e)
SCALE_LOG2 = SCALE * LOG2E
PENALTY = 1e30
CHUNK = 8
GROUP_A = 5
GROUP_B = 5
PARTS = 4
TERM_ROWS = 8
MIB = 1024 * 1024
F32 = jnp.float32
BF16 = jnp.bfloat16
HBM = pl.BlockSpec(memory_space=pltpu.HBM)
VMEM = pl.BlockSpec(memory_space=pltpu.VMEM)
SMEM = pl.BlockSpec(memory_space=pltpu.SMEM)
QUERY, KEY, VALUE, D_OUT = range(4)


def in_hbm(*arrays):
    return [pltpu.with_memory_space_constraint(a, pltpu.HBM) for a in arrays]


def dot_nn(a, b):
    return lax.dot_general(a, b, (((1,), (0,)), ((), ())), preferred_element_type=F32)


def dot_nt(a, b):
    return lax.dot_general(a, b, (((1,), (1,)), ((), ())), preferred_element_type=F32)


def dot_tn(a, b):
    return lax.dot_general(a, b, (((0,), (0,)), ((), ())), preferred_element_type=F32)


def slot_of(wide, t):
    return wide[:, t * BLOCK : (t + 1) * BLOCK]


def lane_fold(combine, wide):
    return functools.reduce(combine, [slot_of(wide, t) for t in range(wide.shape[1] // BLOCK)])


def row_sum(a):
    return jnp.sum(a, axis=1, keepdims=True)


def loop(count, body, start, unroll=True):
    return lax.fori_loop(0, count, body, start, unroll=unroll)


def key_slots(i, width_ref, global_ref, random_ref, block_count):
    wide = width_ref[0] >= 1
    ids = [i]
    penalties = [jnp.float32(0.0)]
    candidates = [(i - 1, wide & (i > 0)), (i + 1, wide & (i < block_count - 1))]
    candidates += [(global_ref[0, n], None) for n in range(2)]
    candidates += [(random_ref[0, i, n], None) for n in range(random_ref.shape[2])]
    for block_id, listed in candidates:
        unusable = functools.reduce(jnp.logical_or, [block_id == t for t in ids])
        if listed is not None:
            unusable = unusable | jnp.logical_not(listed)
        ids.append(jnp.where(unusable, i, block_id))
        penalties.append(jnp.where(unusable, jnp.float32(PENALTY), jnp.float32(0.0)))
    return ids, penalties


def sparse_blocks(step, group, global_ref):
    low = jnp.minimum(global_ref[0, 0], global_ref[0, 1])
    high = jnp.maximum(global_ref[0, 0], global_ref[0, 1])
    blocks = []
    for u in range(group):
        n = step * group + u
        i = n + (n >= low).astype(jnp.int32)
        blocks.append(i + (i >= high).astype(jnp.int32))
    return blocks


def load_all(x_hbm, x_ref, sems):
    copies = [pltpu.make_async_copy(x_hbm.at[:, n], x_ref.at[n], sems.at[n]) for n in range(4)]
    for n in (KEY, QUERY, VALUE, D_OUT):
        copies[n].start()
    return copies


def scale_keys(x_ref, ks_ref, gain_k):
    def body(j, carry):
        ks_ref[j] = (x_ref[KEY, j].astype(F32) * gain_k).astype(BF16)
        return carry

    loop(ks_ref.shape[0], body, 0, 8)


def pair(ref, g0, g1):
    return jnp.concatenate([ref[g0], ref[g1]], 0)


def chunk_of(ref, c):
    return ref[pl.ds(c * CHUNK, CHUNK)].reshape(CHUNK * BLOCK, HD)


def forward_kernel(
    width_ref, global_ref, random_ref, x_hbm, gain_ref, y_hbm, lse_hbm,
    x_ref, ks_ref, p_ref, dv_ref, y_ref, lse_ref, in_sems, out_sems, lse_sem,
):
    copies = load_all(x_hbm, x_ref, in_sems)
    block_count = ks_ref.shape[0]
    chunks = block_count // CHUNK
    gain_q = gain_ref[0:1, :]
    g0 = global_ref[0, 0]
    g1 = global_ref[0, 1]
    k_raw, v_ref, q_ref, d_ref = (x_ref.at[n] for n in (KEY, VALUE, QUERY, D_OUT))
    copies[KEY].wait()
    scale_keys(x_ref, ks_ref, gain_ref[1:2, :])
    copies[QUERY].wait()

    q_scaled = (pair(q_ref, g0, g1).astype(F32) * gain_q).astype(BF16)
    rows = 2 * BLOCK

    def full_scores(c, top):
        scores = dot_nt(q_scaled, chunk_of(ks_ref, c))
        p_ref[c] = scores
        return jnp.maximum(top, lane_fold(jnp.maximum, scores))

    top = loop(chunks, full_scores, jnp.full((rows, BLOCK), -3e38, F32))
    top = jnp.max(top, axis=1, keepdims=True) * SCALE_LOG2

    def full_exp(c, total):
        e = jnp.exp2(p_ref[c] * SCALE_LOG2 - top)
        p_ref[c] = e
        return total + lane_fold(jnp.add, e)

    total = row_sum(loop(chunks, full_exp, jnp.zeros((rows, BLOCK), F32)))
    inverse = 1.0 / total
    lse = jnp.broadcast_to(top + jnp.log(total) * LOG2E, (rows, BLOCK))
    lse_ref[g0] = lse[:BLOCK]
    lse_ref[g1] = lse[BLOCK:]
    copies[VALUE].wait()
    copies[D_OUT].wait()
    d_out = pair(d_ref, g0, g1)

    def full_out(c, acc):
        p_b = (p_ref[c] * inverse).astype(BF16)
        dv_t = dot_tn(d_out, p_b)
        for n in range(CHUNK):
            dv_ref[c * CHUNK + n] = slot_of(dv_t, n)
        return acc + dot_nn(p_b, chunk_of(v_ref, c))

    out = loop(chunks, full_out, jnp.zeros((rows, HD), F32)).astype(BF16)
    y_ref[g0, 0] = out[:BLOCK]
    y_ref[g1, 0] = out[BLOCK:]

    def step(n, carry):
        blocks = sparse_blocks(n, GROUP_A, global_ref)
        us = range(GROUP_A)
        slots = [key_slots(i, width_ref, global_ref, random_ref, block_count) for i in blocks]
        k_slots = [jnp.concatenate([ks_ref[t] for t in slots[u][0]], 0) for u in us]
        v_slots = [jnp.concatenate([v_ref[t] for t in slots[u][0]], 0) for u in us]
        q_scaled = [(q_ref[i].astype(F32) * gain_q).astype(BF16) for i in blocks]
        d_out = [d_ref[i] for i in blocks]
        scores = [dot_nt(q_scaled[u], k_slots[u]) for u in us]
        tops = [
            jnp.max(lane_fold(jnp.maximum, scores[u]), axis=1, keepdims=True) * SCALE_LOG2
            for u in us
        ]
        es = [
            [
                jnp.exp2(slot_of(scores[u], t) * SCALE_LOG2 - (tops[u] + penalty))
                for t, penalty in enumerate(slots[u][1])
            ]
            for u in us
        ]
        totals = [row_sum(functools.reduce(jnp.add, es[u])) for u in us]
        inverses = [1.0 / totals[u] for u in us]
        p_b = [jnp.concatenate([(e * inverses[u]).astype(BF16) for e in es[u]], 1) for u in us]
        outs = [dot_nn(p_b[u], v_slots[u]).astype(BF16) for u in us]
        dv_t = [dot_tn(d_out[u], p_b[u]) for u in us]
        for u in us:
            y_ref[blocks[u], 0] = outs[u]
            lse_ref[blocks[u]] = jnp.broadcast_to(tops[u] + jnp.log(totals[u]) * LOG2E, (BLOCK, BLOCK))
        for u in us:
            for t, block_id in enumerate(slots[u][0]):
                dv_ref[block_id] += slot_of(dv_t[u], t)
        return carry

    lax.fori_loop(0, (block_count - 2) // GROUP_A, step, 0)

    lse_copy = pltpu.make_async_copy(lse_ref, lse_hbm, lse_sem)
    lse_copy.start()

    def finish(j, carry):
        y_ref[j, 1] = dv_ref[j].T.astype(BF16)
        return carry

    out_copies = []
    for part in range(PARTS):
        size = block_count // PARTS
        lax.fori_loop(part * size, (part + 1) * size, finish, 0, unroll=True)
        rows = pl.ds(part * size, size)
        out_copies.append(pltpu.make_async_copy(y_ref.at[rows], y_hbm.at[rows], out_sems.at[part]))
        out_copies[-1].start()
    for copy in out_copies:
        copy.wait()
    lse_copy.wait()


def backward_kernel(
    width_ref, global_ref, random_ref, x_hbm, gain_ref, lse_hbm, out_hbm, y_hbm, terms_ref,
    x_ref, ks_ref, lse_ref, out_ref, dk_ref, y_ref, tq_ref, in_sems, out_sems, lse_sem, o_sem,
):
    copies = load_all(x_hbm, x_ref, in_sems)
    lse_copy = pltpu.make_async_copy(lse_hbm, lse_ref, lse_sem)
    lse_copy.start()
    out_copy = pltpu.make_async_copy(out_hbm.at[:, 0], out_ref, o_sem)
    out_copy.start()
    block_count = ks_ref.shape[0]
    chunks = block_count // CHUNK
    gain_q = gain_ref[0:1, :]
    gain_k = gain_ref[1:2, :]
    g0 = global_ref[0, 0]
    g1 = global_ref[0, 1]
    k_raw, v_ref, q_ref, d_ref = (x_ref.at[n] for n in (KEY, VALUE, QUERY, D_OUT))
    copies[KEY].wait()
    scale_keys(x_ref, ks_ref, gain_k)
    copies[QUERY].wait()
    q_raw = pair(q_ref, g0, g1).astype(F32)
    q_scaled = (q_raw * gain_q).astype(BF16)
    lse_copy.wait()
    lse = jnp.concatenate([pair(lse_ref, g0, g1)] * CHUNK, 1)
    copies[VALUE].wait()
    copies[D_OUT].wait()
    out_copy.wait()
    d_out = pair(d_ref, g0, g1)
    row_dot = row_sum(d_out.astype(F32) * pair(out_ref, g0, g1).astype(F32))

    def full_back(c, acc):
        keys = chunk_of(ks_ref, c)
        p = jnp.exp2(dot_nt(q_scaled, keys) * SCALE_LOG2 - lse)
        ds = (p * (dot_nt(d_out, chunk_of(v_ref, c)) - row_dot)).astype(BF16)
        dk_t = dot_tn(q_scaled, ds)
        for n in range(CHUNK):
            dk_ref[c * CHUNK + n] = slot_of(dk_t, n)
        return acc + dot_nn(ds, keys)

    dq = loop(chunks, full_back, jnp.zeros((2 * BLOCK, HD), F32)) * SCALE
    dq_b = (dq * gain_q).astype(BF16)
    y_ref[g0, 0] = dq_b[:BLOCK]
    y_ref[g1, 0] = dq_b[BLOCK:]
    terms = dq * q_raw
    tq_ref[...] = terms[:BLOCK] + terms[BLOCK:]

    def step(n, carry):
        blocks = sparse_blocks(n, GROUP_B, global_ref)
        us = range(GROUP_B)
        slots = [key_slots(i, width_ref, global_ref, random_ref, block_count) for i in blocks]
        k_slots = [jnp.concatenate([ks_ref[t] for t in slots[u][0]], 0) for u in us]
        v_slots = [jnp.concatenate([v_ref[t] for t in slots[u][0]], 0) for u in us]
        q_raw = [q_ref[i].astype(F32) for i in blocks]
        q_scaled = [(q * gain_q).astype(BF16) for q in q_raw]
        d_out = [d_ref[i] for i in blocks]
        scores = [dot_nt(q_scaled[u], k_slots[u]) for u in us]
        dps = [dot_nt(d_out[u], v_slots[u]) for u in us]
        row_dots = [
            row_sum(d_out[u].astype(F32) * out_ref[blocks[u]].astype(F32)) for u in us
        ]
        ds = []
        for u in us:
            lse = lse_ref[blocks[u]]
            parts = []
            for t, penalty in enumerate(slots[u][1]):
                p = jnp.exp2(slot_of(scores[u], t) * SCALE_LOG2 - (lse + penalty))
                parts.append((p * (slot_of(dps[u], t) - row_dots[u])).astype(BF16))
            ds.append(jnp.concatenate(parts, 1))
        dqs = [dot_nn(ds[u], k_slots[u]) * SCALE for u in us]
        dk_t = [dot_tn(q_scaled[u], ds[u]) for u in us]
        for u in us:
            y_ref[blocks[u], 0] = (dqs[u] * gain_q).astype(BF16)
        tq_ref[...] += functools.reduce(jnp.add, [dqs[u] * q_raw[u] for u in us])
        for u in us:
            for t, block_id in enumerate(slots[u][0]):
                dk_ref[block_id] += slot_of(dk_t[u], t)
        return carry

    lax.fori_loop(0, (block_count - 2) // GROUP_B, step, 0)

    def finish(j, acc):
        dk = dk_ref[j].T * SCALE
        y_ref[j, 1] = (dk * gain_k).astype(BF16)
        return acc + dk * k_raw[j].astype(F32)

    tk = jnp.zeros((BLOCK, HD), F32)
    size = block_count // PARTS
    out_copies = []
    for part in range(PARTS):
        tk = lax.fori_loop(part * size, (part + 1) * size, finish, tk, unroll=True)
        for n in range(2):
            src = y_ref.at[pl.ds(part * size, size), n]
            dst = y_hbm.at[pl.ds(part * size, size), pl.ds(n * BLOCK, BLOCK)]
            out_copies.append(pltpu.make_async_copy(src, dst, out_sems.at[part, n]))
            out_copies[-1].start()
    terms_ref[0:1, :] = jnp.sum(tq_ref[...], axis=0, keepdims=True)
    terms_ref[1:2, :] = jnp.sum(tk, axis=0, keepdims=True)
    for copy in out_copies:
        copy.wait()


def forward(widths, global_ids, random_ids, x, gains):
    blocks = x.shape[0]
    return pl.pallas_call(
        forward_kernel,
        out_shape=(
            pltpu.HBM((blocks, 2, BLOCK, HD), BF16),
            pltpu.HBM((blocks, BLOCK, BLOCK), F32),
        ),
        in_specs=[SMEM, SMEM, SMEM, HBM, VMEM],
        out_specs=(HBM, HBM),
        scratch_shapes=[
            pltpu.VMEM((4, blocks, BLOCK, HD), BF16),
            pltpu.VMEM((blocks, BLOCK, HD), BF16),
            pltpu.VMEM((blocks // CHUNK, 2 * BLOCK, CHUNK * BLOCK), F32),
            pltpu.VMEM((blocks, HD, BLOCK), F32),
            pltpu.VMEM((blocks, 2, BLOCK, HD), BF16),
            pltpu.VMEM((blocks, BLOCK, BLOCK), F32),
            pltpu.SemaphoreType.DMA((4,)),
            pltpu.SemaphoreType.DMA((PARTS,)),
            pltpu.SemaphoreType.DMA,
        ],
        compiler_params=pltpu.CompilerParams(vmem_limit_bytes=36 * MIB),
        name="attention_forward",
    )(widths, global_ids, random_ids, *in_hbm(x), gains)


def backward(widths, global_ids, random_ids, x, gains, lse, y):
    blocks = x.shape[0]
    return pl.pallas_call(
        backward_kernel,
        out_shape=(
            pltpu.HBM((blocks, 2 * BLOCK + TERM_ROWS, HD), BF16),
            jax.ShapeDtypeStruct((2, HD), F32),
        ),
        in_specs=[SMEM, SMEM, SMEM, HBM, VMEM, HBM, HBM],
        out_specs=(HBM, VMEM),
        scratch_shapes=[
            pltpu.VMEM((4, blocks, BLOCK, HD), BF16),
            pltpu.VMEM((blocks, BLOCK, HD), BF16),
            pltpu.VMEM((blocks, BLOCK, BLOCK), F32),
            pltpu.VMEM((blocks, BLOCK, HD), BF16),
            pltpu.VMEM((blocks, HD, BLOCK), F32),
            pltpu.VMEM((blocks, 2, BLOCK, HD), BF16),
            pltpu.VMEM((BLOCK, HD), F32),
            pltpu.SemaphoreType.DMA((4,)),
            pltpu.SemaphoreType.DMA((PARTS, 2)),
            pltpu.SemaphoreType.DMA,
            pltpu.SemaphoreType.DMA,
        ],
        compiler_params=pltpu.CompilerParams(vmem_limit_bytes=36 * MIB),
        name="attention_backward",
    )(widths, global_ids, random_ids, *in_hbm(x), gains, *in_hbm(lse, y))


def put_terms_kernel(y_in, total_ref, y_out, rows_ref, sem):
    total = total_ref[...]
    high = total.astype(BF16)
    low = (total - high.astype(F32)).astype(BF16)
    rows = jnp.concatenate([high, low, jnp.zeros((TERM_ROWS - 4, HD), BF16)], 0)
    rows_ref[...] = jnp.broadcast_to(rows[None], rows_ref.shape)
    copy = pltpu.make_async_copy(rows_ref, y_out.at[:, pl.ds(2 * BLOCK, TERM_ROWS)], sem)
    copy.start()
    copy.wait()


def put_terms(y, total):
    return pl.pallas_call(
        put_terms_kernel,
        out_shape=pltpu.HBM(y.shape, y.dtype),
        in_specs=[HBM, VMEM],
        out_specs=HBM,
        scratch_shapes=[
            pltpu.VMEM((y.shape[0], TERM_ROWS, HD), BF16),
            pltpu.SemaphoreType.DMA,
        ],
        input_output_aliases={0: 0},
        name="put_terms",
    )(*in_hbm(y), total)


def split_kernel(q_hbm, k_hbm, v_hbm, d_hbm, x_hbm, in_ref, x_ref, in_sems, out_sems):
    sources = (q_hbm, k_hbm, v_hbm, d_hbm)
    heads = x_ref.shape[0] // PARTS
    width = heads * HD

    def fetch(c, n):
        src = sources[n].at[0, :, pl.ds(c * width, width)]
        return pltpu.make_async_copy(src, in_ref.at[c, n], in_sems.at[c, n])

    def send(c):
        part = pl.ds(c * heads, heads)
        return pltpu.make_async_copy(x_ref.at[part], x_hbm.at[part], out_sems.at[c])

    for c in range(PARTS):
        for n in range(4):
            fetch(c, n).start()
    for c in range(PARTS):
        for n in range(4):
            fetch(c, n).wait()
            for h in range(heads):
                x_ref[c * heads + h, n] = in_ref[c, n, :, h * HD : (h + 1) * HD]
        send(c).start()
    for c in range(PARTS):
        send(c).wait()


def split_heads(arrays):
    _, tokens, channels = arrays[0].shape
    heads = channels // HD
    return pl.pallas_call(
        split_kernel,
        out_shape=pltpu.HBM((heads, 4, tokens, HD), BF16),
        in_specs=[HBM] * 4,
        out_specs=HBM,
        scratch_shapes=[
            pltpu.VMEM((PARTS, 4, tokens, channels // PARTS), BF16),
            pltpu.VMEM((heads, 4, tokens, HD), BF16),
            pltpu.SemaphoreType.DMA((PARTS, 4)),
            pltpu.SemaphoreType.DMA((PARTS,)),
        ],
        compiler_params=pltpu.CompilerParams(vmem_limit_bytes=16 * MIB),
        name="split_heads",
    )(*in_hbm(*arrays))


def join_pair(z_hbm, targets, in_ref, out_ref, in_sems, out_sems):
    heads = in_ref.shape[0] // PARTS
    width = heads * HD

    def fetch(c):
        part = pl.ds(c * heads, heads)
        src = z_hbm.at[part, pl.ds(0, 2 * BLOCK)]
        return pltpu.make_async_copy(src, in_ref.at[part], in_sems.at[c])

    def send(c, n):
        dst = targets[n].at[0, :, pl.ds(c * width, width)]
        return pltpu.make_async_copy(out_ref.at[c, n], dst, out_sems.at[c, n])

    for c in range(PARTS):
        fetch(c).start()
    for c in range(PARTS):
        fetch(c).wait()
        for n in range(2):
            for h in range(heads):
                rows = in_ref[c * heads + h, n * BLOCK : (n + 1) * BLOCK]
                out_ref[c, n, :, h * HD : (h + 1) * HD] = rows
            send(c, n).start()
    for c in range(PARTS):
        for n in range(2):
            send(c, n).wait()


def join_kernel(z_hbm, a_hbm, b_hbm, in_ref, out_ref, in_sems, out_sems):
    join_pair(z_hbm, (a_hbm, b_hbm), in_ref, out_ref, in_sems, out_sems)


def join_terms_kernel(place_ref, z_ref, a_hbm, b_hbm, gains_ref, out_ref, out_sems):
    targets = (a_hbm, b_hbm)
    heads = z_ref.shape[0] // PARTS
    width = heads * HD
    copies = []
    for c in range(PARTS):
        for n in range(2):
            for h in range(heads):
                rows = z_ref[c * heads + h, n * BLOCK : (n + 1) * BLOCK]
                out_ref[c, n, :, h * HD : (h + 1) * HD] = rows
            dst = targets[n].at[0, :, pl.ds(c * width, width)]
            copies.append(pltpu.make_async_copy(out_ref.at[c, n], dst, out_sems.at[c, n]))
            copies[-1].start()
    own = gains_ref.shape[1] // HD
    for n in range(own):
        rows = z_ref[place_ref[0] * own + n, 2 * BLOCK : 2 * BLOCK + TERM_ROWS].astype(F32)
        gains_ref[:, n * HD : (n + 1) * HD] = rows[0:2] + rows[2:4]
    for copy in copies:
        copy.wait()


def join_scratch(heads, tokens):
    return [
        pltpu.VMEM((heads, 2 * tokens, HD), BF16),
        pltpu.VMEM((PARTS, 2, tokens, heads * HD // PARTS), BF16),
    ], [
        pltpu.SemaphoreType.DMA((PARTS,)),
        pltpu.SemaphoreType.DMA((PARTS, 2)),
    ]


def join_heads(z):
    heads = z.shape[0]
    buffers, sems = join_scratch(heads, BLOCK)
    return pl.pallas_call(
        join_kernel,
        out_shape=(pltpu.HBM((1, BLOCK, heads * HD), BF16),) * 2,
        in_specs=[HBM],
        out_specs=(HBM,) * 2,
        scratch_shapes=buffers + sems,
        compiler_params=pltpu.CompilerParams(vmem_limit_bytes=16 * MIB),
        name="join_heads",
    )(*in_hbm(z))


def join_heads_terms(place, z, own):
    heads = z.shape[0]
    buffers, sems = join_scratch(heads, BLOCK)
    return pl.pallas_call(
        join_terms_kernel,
        out_shape=(pltpu.HBM((1, BLOCK, heads * HD), BF16),) * 2
        + (jax.ShapeDtypeStruct((2, own * HD), F32),),
        in_specs=[SMEM, VMEM],
        out_specs=(HBM, HBM, VMEM),
        scratch_shapes=buffers[1:] + sems[1:],
        compiler_params=pltpu.CompilerParams(vmem_limit_bytes=16 * MIB),
        name="join_heads_terms",
    )(place, z)


def exchange(x):
    return lax.all_to_all(x, "ctx", split_axis=0, concat_axis=0, tiled=True)


def sum_over_sequences(terms):
    count = lax.axis_size("dp")
    stride = 1
    while stride < count:
        pairs = [(n, n ^ stride) for n in range(count)]
        terms = terms + lax.ppermute(terms, "dp", pairs)
        stride *= 2
    return terms


def on_device(queries, keys, values, d_out, gains, window_widths, global_blocks, random_blocks):
    x = exchange(split_heads((queries, keys, values, d_out)))
    all_gains = lax.all_gather(gains, "dp", axis=1, tiled=True)
    own_gains = lax.dynamic_slice_in_dim(all_gains, lax.axis_index("ctx") * HD, HD, 1)
    tables = (window_widths, global_blocks, random_blocks)
    out_dv, lse = forward(*tables, x, own_gains)
    back_out_dv = exchange(out_dv.reshape(-1, 2 * BLOCK, HD))
    dq_dk, terms = backward(*tables, x, own_gains, lse, out_dv)
    dq_dk = put_terms(dq_dk, sum_over_sequences(terms))
    out, d_values = join_heads(back_out_dv)
    place = lax.axis_index("dp").reshape(1)
    d_queries, d_keys, d_gains = join_heads_terms(place, exchange(dq_dk), gains.shape[1] // HD)
    return (out, d_queries, d_keys, d_values, d_gains)


def solution(mesh):
    tokens = P("dp", "ctx", None)
    return jax.shard_map(
        on_device,
        mesh=mesh,
        in_specs=(
            tokens, tokens, tokens, tokens,
            P(None, "dp"), P("ctx"), P("dp", None), P("dp", None, None),
        ),
        out_specs=(tokens, tokens, tokens, tokens, P(None, "dp")),
        check_vma=False,
    )
```

```python
import functools
import math

import jax
import jax.numpy as jnp
from jax import lax
from jax.experimental import pallas as pl
from jax.experimental.pallas import tpu as pltpu
from jax.sharding import PartitionSpec as P

HD = 128
BLOCK = 128
SCALE = 1.0 / math.sqrt(HD)
LOG2E = math.log2(math.e)
SCALE_LOG2 = SCALE * LOG2E
PENALTY = 1e30
CHUNK = 8
GROUP = 5
PARTS = 4
TERM_ROWS = 8
MIB = 1024 * 1024
F32 = jnp.float32
BF16 = jnp.bfloat16
HBM = pl.BlockSpec(memory_space=pltpu.HBM)
VMEM = pl.BlockSpec(memory_space=pltpu.VMEM)
SMEM = pl.BlockSpec(memory_space=pltpu.SMEM)
QUERY, KEY, VALUE, D_OUT = range(4)


def in_hbm(*arrays):
    return [pltpu.with_memory_space_constraint(a, pltpu.HBM) for a in arrays]


def dot_nn(a, b):
    return lax.dot_general(a, b, (((1,), (0,)), ((), ())), preferred_element_type=F32)


def dot_nt(a, b):
    return lax.dot_general(a, b, (((1,), (1,)), ((), ())), preferred_element_type=F32)


def dot_tn(a, b):
    return lax.dot_general(a, b, (((0,), (0,)), ((), ())), preferred_element_type=F32)


def slot_of(wide, t):
    return wide[:, t * BLOCK : (t + 1) * BLOCK]


def lane_fold(combine, wide):
    return functools.reduce(combine, [slot_of(wide, t) for t in range(wide.shape[1] // BLOCK)])


def row_sum(a):
    return jnp.sum(a, axis=1, keepdims=True)


def loop(count, body, start, unroll=True):
    return lax.fori_loop(0, count, body, start, unroll=unroll)


def key_slots(i, width_ref, global_ref, random_ref, block_count):
    wide = width_ref[0] >= 1
    ids = [i]
    penalties = [jnp.float32(0.0)]
    candidates = [(i - 1, wide & (i > 0)), (i + 1, wide & (i < block_count - 1))]
    candidates += [(global_ref[0, n], None) for n in range(2)]
    candidates += [(random_ref[0, i, n], None) for n in range(random_ref.shape[2])]
    for block_id, listed in candidates:
        unusable = functools.reduce(jnp.logical_or, [block_id == t for t in ids])
        if listed is not None:
            unusable = unusable | jnp.logical_not(listed)
        ids.append(jnp.where(unusable, i, block_id))
        penalties.append(jnp.where(unusable, jnp.float32(PENALTY), jnp.float32(0.0)))
    return ids, penalties


def sparse_blocks(step, group, global_ref):
    low = jnp.minimum(global_ref[0, 0], global_ref[0, 1])
    high = jnp.maximum(global_ref[0, 0], global_ref[0, 1])
    blocks = []
    for u in range(group):
        n = step * group + u
        i = n + (n >= low).astype(jnp.int32)
        blocks.append(i + (i >= high).astype(jnp.int32))
    return blocks


def load_all(x_hbm, x_ref, sems):
    copies = [pltpu.make_async_copy(x_hbm.at[:, n], x_ref.at[n], sems.at[n]) for n in range(4)]
    for n in (KEY, QUERY, VALUE, D_OUT):
        copies[n].start()
    return copies


def scale_keys(x_ref, ks_ref, gain_k):
    def body(j, carry):
        ks_ref[j] = (x_ref[KEY, j].astype(F32) * gain_k).astype(BF16)
        return carry

    loop(ks_ref.shape[0], body, 0, 8)


def pair(ref, g0, g1):
    return jnp.concatenate([ref[g0], ref[g1]], 0)


def chunk_of(ref, c):
    return ref[pl.ds(c * CHUNK, CHUNK)].reshape(CHUNK * BLOCK, HD)


def main_kernel(
    width_ref, global_ref, random_ref, x_hbm, gain_ref, y_hbm, lse_hbm, terms_ref,
    x_ref, ks_ref, p_ref, dk_ref, y_ref, lse_ref, tq_ref, in_sems, out_sems, lse_sem,
):
    copies = load_all(x_hbm, x_ref, in_sems)
    block_count = ks_ref.shape[0]
    chunks = block_count // CHUNK
    gain_q = gain_ref[0:1, :]
    gain_k = gain_ref[1:2, :]
    g0 = global_ref[0, 0]
    g1 = global_ref[0, 1]
    k_raw, v_ref, q_ref, d_ref = (x_ref.at[n] for n in (KEY, VALUE, QUERY, D_OUT))
    copies[KEY].wait()
    scale_keys(x_ref, ks_ref, gain_k)
    copies[QUERY].wait()

    q_raw = pair(q_ref, g0, g1).astype(F32)
    q_scaled = (q_raw * gain_q).astype(BF16)
    rows = 2 * BLOCK

    def full_scores(c, top):
        scores = dot_nt(q_scaled, chunk_of(ks_ref, c))
        p_ref[c] = scores
        return jnp.maximum(top, lane_fold(jnp.maximum, scores))

    top = loop(chunks, full_scores, jnp.full((rows, BLOCK), -3e38, F32))
    top = jnp.max(top, axis=1, keepdims=True) * SCALE_LOG2

    def full_exp(c, total):
        e = jnp.exp2(p_ref[c] * SCALE_LOG2 - top)
        p_ref[c] = e
        return total + lane_fold(jnp.add, e)

    total = row_sum(loop(chunks, full_exp, jnp.zeros((rows, BLOCK), F32)))
    inverse = 1.0 / total
    lse = jnp.broadcast_to(top + jnp.log(total) * LOG2E, (rows, BLOCK))
    lse_ref[g0] = lse[:BLOCK]
    lse_ref[g1] = lse[BLOCK:]
    copies[VALUE].wait()
    copies[D_OUT].wait()
    d_out = pair(d_ref, g0, g1)

    def full_out(c, acc):
        p = p_ref[c] * inverse
        p_ref[c] = p
        return acc + dot_nn(p.astype(BF16), chunk_of(v_ref, c))

    out = loop(chunks, full_out, jnp.zeros((rows, HD), F32)).astype(BF16)
    y_ref[g0, 0] = out[:BLOCK]
    y_ref[g1, 0] = out[BLOCK:]
    row_dot = row_sum(d_out.astype(F32) * out.astype(F32))

    def full_back(c, acc):
        ds = (p_ref[c] * (dot_nt(d_out, chunk_of(v_ref, c)) - row_dot)).astype(BF16)
        dk_t = dot_tn(q_scaled, ds)
        for n in range(CHUNK):
            dk_ref[c * CHUNK + n] = slot_of(dk_t, n)
        return acc + dot_nn(ds, chunk_of(ks_ref, c))

    dq = loop(chunks, full_back, jnp.zeros((rows, HD), F32)) * SCALE
    dq_b = (dq * gain_q).astype(BF16)
    y_ref[g0, 1] = dq_b[:BLOCK]
    y_ref[g1, 1] = dq_b[BLOCK:]
    terms = dq * q_raw
    tq_ref[...] = terms[:BLOCK] + terms[BLOCK:]

    def step(n, carry):
        blocks = sparse_blocks(n, GROUP, global_ref)
        us = range(GROUP)
        slots = [key_slots(i, width_ref, global_ref, random_ref, block_count) for i in blocks]
        k_slots = [jnp.concatenate([ks_ref[t] for t in slots[u][0]], 0) for u in us]
        v_slots = [jnp.concatenate([v_ref[t] for t in slots[u][0]], 0) for u in us]
        q_raw = [q_ref[i].astype(F32) for i in blocks]
        q_scaled = [(q * gain_q).astype(BF16) for q in q_raw]
        d_out = [d_ref[i] for i in blocks]
        scores = [dot_nt(q_scaled[u], k_slots[u]) for u in us]
        dps = [dot_nt(d_out[u], v_slots[u]) for u in us]
        tops = [
            jnp.max(lane_fold(jnp.maximum, scores[u]), axis=1, keepdims=True) * SCALE_LOG2
            for u in us
        ]
        es = [
            [
                jnp.exp2(slot_of(scores[u], t) * SCALE_LOG2 - (tops[u] + penalty))
                for t, penalty in enumerate(slots[u][1])
            ]
            for u in us
        ]
        totals = [row_sum(functools.reduce(jnp.add, es[u])) for u in us]
        inverses = [1.0 / totals[u] for u in us]
        ps = [[e * inverses[u] for e in es[u]] for u in us]
        p_b = [jnp.concatenate([p.astype(BF16) for p in ps[u]], 1) for u in us]
        outs = [dot_nn(p_b[u], v_slots[u]).astype(BF16) for u in us]
        row_dots = [row_sum(d_out[u].astype(F32) * outs[u].astype(F32)) for u in us]
        ds = [
            jnp.concatenate(
                [
                    (p * (slot_of(dps[u], t) - row_dots[u])).astype(BF16)
                    for t, p in enumerate(ps[u])
                ],
                1,
            )
            for u in us
        ]
        dqs = [dot_nn(ds[u], k_slots[u]) * SCALE for u in us]
        dk_t = [dot_tn(q_scaled[u], ds[u]) for u in us]
        for u in us:
            y_ref[blocks[u], 0] = outs[u]
            y_ref[blocks[u], 1] = (dqs[u] * gain_q).astype(BF16)
            lse_ref[blocks[u]] = jnp.broadcast_to(
                tops[u] + jnp.log(totals[u]) * LOG2E, (BLOCK, BLOCK)
            )
        tq_ref[...] += functools.reduce(jnp.add, [dqs[u] * q_raw[u] for u in us])
        for u in us:
            for t, block_id in enumerate(slots[u][0]):
                dk_ref[block_id] += slot_of(dk_t[u], t)
        return carry

    lax.fori_loop(0, (block_count - 2) // GROUP, step, 0)
    lse_copy = pltpu.make_async_copy(lse_ref, lse_hbm, lse_sem)

    def finish(j, acc):
        dk = dk_ref[j].T * SCALE
        y_ref[j, 2] = (dk * gain_k).astype(BF16)
        return acc + dk * k_raw[j].astype(F32)

    tk = jnp.zeros((BLOCK, HD), F32)
    size = block_count // PARTS
    out_copies = []
    for part in range(PARTS):
        tk = lax.fori_loop(part * size, (part + 1) * size, finish, tk, unroll=True)
        rows = pl.ds(part * size, size)
        out_copies.append(pltpu.make_async_copy(y_ref.at[rows], y_hbm.at[rows], out_sems.at[part]))
        out_copies[-1].start()
    lse_copy.start()
    terms_ref[0:1, :] = jnp.sum(tq_ref[...], axis=0, keepdims=True)
    terms_ref[1:2, :] = jnp.sum(tk, axis=0, keepdims=True)
    for copy in out_copies:
        copy.wait()
    lse_copy.wait()


def values_kernel(
    width_ref, global_ref, random_ref, x_hbm, gain_ref, lse_hbm, y_hbm,
    x_ref, ks_ref, lse_ref, dv_ref, y_ref, in_sems, lse_sem, out_sem,
):
    lse_copy = pltpu.make_async_copy(lse_hbm, lse_ref, lse_sem)
    lse_copy.start()
    copies = [
        pltpu.make_async_copy(x_hbm.at[:, n], x_ref.at[n], in_sems.at[n])
        for n in (KEY, QUERY, D_OUT)
    ]
    for copy in copies:
        copy.start()
    block_count = ks_ref.shape[0]
    chunks = block_count // CHUNK
    gain_q = gain_ref[0:1, :]
    g0 = global_ref[0, 0]
    g1 = global_ref[0, 1]
    q_ref, d_ref = x_ref.at[QUERY], x_ref.at[D_OUT]
    lse_copy.wait()
    for copy in copies:
        copy.wait()
    scale_keys(x_ref, ks_ref, gain_ref[1:2, :])
    q_scaled = (pair(q_ref, g0, g1).astype(F32) * gain_q).astype(BF16)
    lse = jnp.concatenate([pair(lse_ref, g0, g1)] * CHUNK, 1)
    d_out = pair(d_ref, g0, g1)

    def full_values(c, carry):
        scores = dot_nt(q_scaled, chunk_of(ks_ref, c))
        dv_t = dot_tn(d_out, jnp.exp2(scores * SCALE_LOG2 - lse).astype(BF16))
        for n in range(CHUNK):
            dv_ref[c * CHUNK + n] = slot_of(dv_t, n)
        return carry

    loop(chunks, full_values, 0)

    def step(n, carry):
        blocks = sparse_blocks(n, GROUP, global_ref)
        us = range(GROUP)
        slots = [key_slots(i, width_ref, global_ref, random_ref, block_count) for i in blocks]
        k_slots = [jnp.concatenate([ks_ref[t] for t in slots[u][0]], 0) for u in us]
        q_scaled = [(q_ref[i].astype(F32) * gain_q).astype(BF16) for i in blocks]
        scores = [dot_nt(q_scaled[u], k_slots[u]) for u in us]
        dv_t = []
        for u in us:
            lse = lse_ref[blocks[u]]
            p_b = [
                jnp.exp2(slot_of(scores[u], t) * SCALE_LOG2 - (lse + penalty)).astype(BF16)
                for t, penalty in enumerate(slots[u][1])
            ]
            dv_t.append(dot_tn(d_ref[blocks[u]], jnp.concatenate(p_b, 1)))
        for u in us:
            for t, block_id in enumerate(slots[u][0]):
                dv_ref[block_id] += slot_of(dv_t[u], t)
        return carry

    lax.fori_loop(0, (block_count - 2) // GROUP, step, 0)

    def finish(j, carry):
        y_ref[j] = dv_ref[j].T.astype(BF16)
        return carry

    loop(block_count, finish, 0, 8)
    copy = pltpu.make_async_copy(y_ref, y_hbm.at[:, pl.ds(0, BLOCK)], out_sem)
    copy.start()
    copy.wait()


def attend_without_values(widths, global_ids, random_ids, x, gains):
    blocks = x.shape[0]
    return pl.pallas_call(
        main_kernel,
        out_shape=(
            pltpu.HBM((blocks, 3, BLOCK, HD), BF16),
            pltpu.HBM((blocks, BLOCK, BLOCK), F32),
            jax.ShapeDtypeStruct((2, HD), F32),
        ),
        in_specs=[SMEM, SMEM, SMEM, HBM, VMEM],
        out_specs=(HBM, HBM, VMEM),
        scratch_shapes=[
            pltpu.VMEM((4, blocks, BLOCK, HD), BF16),
            pltpu.VMEM((blocks, BLOCK, HD), BF16),
            pltpu.VMEM((blocks // CHUNK, 2 * BLOCK, CHUNK * BLOCK), F32),
            pltpu.VMEM((blocks, HD, BLOCK), F32),
            pltpu.VMEM((blocks, 3, BLOCK, HD), BF16),
            pltpu.VMEM((blocks, BLOCK, BLOCK), F32),
            pltpu.VMEM((BLOCK, HD), F32),
            pltpu.SemaphoreType.DMA((4,)),
            pltpu.SemaphoreType.DMA((PARTS,)),
            pltpu.SemaphoreType.DMA,
        ],
        compiler_params=pltpu.CompilerParams(vmem_limit_bytes=40 * MIB),
        name="attend_without_values",
    )(widths, global_ids, random_ids, *in_hbm(x), gains)


def value_gradients(widths, global_ids, random_ids, x, gains, lse):
    blocks = x.shape[0]
    return pl.pallas_call(
        values_kernel,
        out_shape=pltpu.HBM((blocks, BLOCK + TERM_ROWS, HD), BF16),
        in_specs=[SMEM, SMEM, SMEM, HBM, VMEM, HBM],
        out_specs=HBM,
        scratch_shapes=[
            pltpu.VMEM((4, blocks, BLOCK, HD), BF16),
            pltpu.VMEM((blocks, BLOCK, HD), BF16),
            pltpu.VMEM((blocks, BLOCK, BLOCK), F32),
            pltpu.VMEM((blocks, HD, BLOCK), F32),
            pltpu.VMEM((blocks, BLOCK, HD), BF16),
            pltpu.SemaphoreType.DMA((4,)),
            pltpu.SemaphoreType.DMA,
            pltpu.SemaphoreType.DMA,
        ],
        compiler_params=pltpu.CompilerParams(vmem_limit_bytes=40 * MIB),
        name="value_gradients",
    )(widths, global_ids, random_ids, *in_hbm(x), gains, *in_hbm(lse))


def put_terms_kernel(y_in, total_ref, y_out, rows_ref, sem):
    total = total_ref[...]
    high = total.astype(BF16)
    low = (total - high.astype(F32)).astype(BF16)
    rows = jnp.concatenate([high, low, jnp.zeros((TERM_ROWS - 4, HD), BF16)], 0)
    rows_ref[...] = jnp.broadcast_to(rows[None], rows_ref.shape)
    copy = pltpu.make_async_copy(rows_ref, y_out.at[:, pl.ds(BLOCK, TERM_ROWS)], sem)
    copy.start()
    copy.wait()


def put_terms(y, total):
    return pl.pallas_call(
        put_terms_kernel,
        out_shape=pltpu.HBM(y.shape, y.dtype),
        in_specs=[HBM, VMEM],
        out_specs=HBM,
        scratch_shapes=[
            pltpu.VMEM((y.shape[0], TERM_ROWS, HD), BF16),
            pltpu.SemaphoreType.DMA,
        ],
        input_output_aliases={0: 0},
        name="put_terms",
    )(*in_hbm(y), total)


def split_kernel(q_hbm, k_hbm, v_hbm, d_hbm, x_hbm, in_ref, x_ref, in_sems, out_sems):
    sources = (q_hbm, k_hbm, v_hbm, d_hbm)
    heads = x_ref.shape[0] // PARTS
    width = heads * HD

    def fetch(c, n):
        src = sources[n].at[0, :, pl.ds(c * width, width)]
        return pltpu.make_async_copy(src, in_ref.at[c, n], in_sems.at[c, n])

    def send(c):
        part = pl.ds(c * heads, heads)
        return pltpu.make_async_copy(x_ref.at[part], x_hbm.at[part], out_sems.at[c])

    for c in range(PARTS):
        for n in range(4):
            fetch(c, n).start()
    for c in range(PARTS):
        for n in range(4):
            fetch(c, n).wait()
            for h in range(heads):
                x_ref[c * heads + h, n] = in_ref[c, n, :, h * HD : (h + 1) * HD]
        send(c).start()
    for c in range(PARTS):
        send(c).wait()


def split_heads(arrays):
    _, tokens, channels = arrays[0].shape
    heads = channels // HD
    return pl.pallas_call(
        split_kernel,
        out_shape=pltpu.HBM((heads, 4, tokens, HD), BF16),
        in_specs=[HBM] * 4,
        out_specs=HBM,
        scratch_shapes=[
            pltpu.VMEM((PARTS, 4, tokens, channels // PARTS), BF16),
            pltpu.VMEM((heads, 4, tokens, HD), BF16),
            pltpu.SemaphoreType.DMA((PARTS, 4)),
            pltpu.SemaphoreType.DMA((PARTS,)),
        ],
        compiler_params=pltpu.CompilerParams(vmem_limit_bytes=16 * MIB),
        name="split_heads",
    )(*in_hbm(*arrays))


def join_kernel(z_hbm, a_hbm, b_hbm, c_hbm, in_ref, out_ref, in_sems, out_sems):
    targets = (a_hbm, b_hbm, c_hbm)
    heads = in_ref.shape[0] // PARTS
    width = heads * HD

    def fetch(c):
        part = pl.ds(c * heads, heads)
        return pltpu.make_async_copy(z_hbm.at[part], in_ref.at[part], in_sems.at[c])

    def send(c, n):
        dst = targets[n].at[0, :, pl.ds(c * width, width)]
        return pltpu.make_async_copy(out_ref.at[c, n], dst, out_sems.at[c, n])

    for c in range(PARTS):
        fetch(c).start()
    for c in range(PARTS):
        fetch(c).wait()
        for n in range(3):
            for h in range(heads):
                out_ref[c, n, :, h * HD : (h + 1) * HD] = in_ref[c * heads + h, n]
            send(c, n).start()
    for c in range(PARTS):
        for n in range(3):
            send(c, n).wait()


def join_terms_kernel(place_ref, z_ref, a_hbm, gains_ref, out_ref, out_sems):
    heads = z_ref.shape[0] // PARTS
    width = heads * HD
    copies = []
    for c in range(PARTS):
        for h in range(heads):
            out_ref[c, :, h * HD : (h + 1) * HD] = z_ref[c * heads + h, 0:BLOCK]
        dst = a_hbm.at[0, :, pl.ds(c * width, width)]
        copies.append(pltpu.make_async_copy(out_ref.at[c], dst, out_sems.at[c]))
        copies[-1].start()
    own = gains_ref.shape[1] // HD
    for n in range(own):
        rows = z_ref[place_ref[0] * own + n, BLOCK : BLOCK + TERM_ROWS].astype(F32)
        gains_ref[:, n * HD : (n + 1) * HD] = rows[0:2] + rows[2:4]
    for copy in copies:
        copy.wait()


def join_heads(z):
    heads = z.shape[0]
    return pl.pallas_call(
        join_kernel,
        out_shape=(pltpu.HBM((1, BLOCK, heads * HD), BF16),) * 3,
        in_specs=[HBM],
        out_specs=(HBM,) * 3,
        scratch_shapes=[
            pltpu.VMEM((heads, 3, BLOCK, HD), BF16),
            pltpu.VMEM((PARTS, 3, BLOCK, heads * HD // PARTS), BF16),
            pltpu.SemaphoreType.DMA((PARTS,)),
            pltpu.SemaphoreType.DMA((PARTS, 3)),
        ],
        compiler_params=pltpu.CompilerParams(vmem_limit_bytes=16 * MIB),
        name="join_heads",
    )(*in_hbm(z))


def join_heads_terms(place, z, own):
    heads = z.shape[0]
    return pl.pallas_call(
        join_terms_kernel,
        out_shape=(
            pltpu.HBM((1, BLOCK, heads * HD), BF16),
            jax.ShapeDtypeStruct((2, own * HD), F32),
        ),
        in_specs=[SMEM, VMEM],
        out_specs=(HBM, VMEM),
        scratch_shapes=[
            pltpu.VMEM((PARTS, BLOCK, heads * HD // PARTS), BF16),
            pltpu.SemaphoreType.DMA((PARTS,)),
        ],
        compiler_params=pltpu.CompilerParams(vmem_limit_bytes=16 * MIB),
        name="join_heads_terms",
    )(place, z)


def exchange(x):
    return lax.all_to_all(x, "ctx", split_axis=0, concat_axis=0, tiled=True)


def sum_over_sequences(terms):
    count = lax.axis_size("dp")
    stride = 1
    while stride < count:
        pairs = [(n, n ^ stride) for n in range(count)]
        terms = terms + lax.ppermute(terms, "dp", pairs)
        stride *= 2
    return terms


def on_device(queries, keys, values, d_out, gains, window_widths, global_blocks, random_blocks):
    x = exchange(split_heads((queries, keys, values, d_out)))
    all_gains = lax.all_gather(gains, "dp", axis=1, tiled=True)
    own_gains = lax.dynamic_slice_in_dim(all_gains, lax.axis_index("ctx") * HD, HD, 1)
    tables = (window_widths, global_blocks, random_blocks)
    y, lse, terms = attend_without_values(*tables, x, own_gains)
    returned = exchange(y)
    d_values = value_gradients(*tables, x, own_gains, lse)
    d_values = put_terms(d_values, sum_over_sequences(terms))
    out, d_queries, d_keys = join_heads(returned)
    place = lax.axis_index("dp").reshape(1)
    d_values, d_gains = join_heads_terms(place, exchange(d_values), gains.shape[1] // HD)
    return (out, d_queries, d_keys, d_values, d_gains)


def solution(mesh):
    tokens = P("dp", "ctx", None)
    return jax.shard_map(
        on_device,
        mesh=mesh,
        in_specs=(
            tokens, tokens, tokens, tokens,
            P(None, "dp"), P("ctx"), P("dp", None), P("dp", None, None),
        ),
        out_specs=(tokens, tokens, tokens, tokens, P(None, "dp")),
        check_vma=False,
    )
```

```python
import functools
import math

import jax
import jax.numpy as jnp
from jax import lax
from jax.experimental import pallas as pl
from jax.experimental.pallas import tpu as pltpu
from jax.sharding import PartitionSpec as P

HD = 128
BLOCK = 128
SCALE = 1.0 / math.sqrt(HD)
LOG2E = math.log2(math.e)
SCALE_LOG2 = SCALE * LOG2E
PENALTY = 1e30
CHUNK = 8
GROUP = 5
PARTS = 4
TERM_ROWS = 8
MIB = 1024 * 1024
F32 = jnp.float32
BF16 = jnp.bfloat16
HBM = pl.BlockSpec(memory_space=pltpu.HBM)
VMEM = pl.BlockSpec(memory_space=pltpu.VMEM)
SMEM = pl.BlockSpec(memory_space=pltpu.SMEM)
QUERY, KEY, VALUE, D_OUT = range(4)


def in_hbm(*arrays):
    return [pltpu.with_memory_space_constraint(a, pltpu.HBM) for a in arrays]


def dot_nn(a, b):
    return lax.dot_general(a, b, (((1,), (0,)), ((), ())), preferred_element_type=F32)


def dot_nt(a, b):
    return lax.dot_general(a, b, (((1,), (1,)), ((), ())), preferred_element_type=F32)


def dot_tn(a, b):
    return lax.dot_general(a, b, (((0,), (0,)), ((), ())), preferred_element_type=F32)


def slot_of(wide, t):
    return wide[:, t * BLOCK : (t + 1) * BLOCK]


def lane_fold(combine, wide):
    return functools.reduce(combine, [slot_of(wide, t) for t in range(wide.shape[1] // BLOCK)])


def row_sum(a):
    return jnp.sum(a, axis=1, keepdims=True)


def loop(count, body, start, unroll=True):
    return lax.fori_loop(0, count, body, start, unroll=unroll)


def key_slots(i, width_ref, global_ref, random_ref, block_count):
    wide = width_ref[0] >= 1
    ids = [i]
    penalties = [jnp.float32(0.0)]
    candidates = [(i - 1, wide & (i > 0)), (i + 1, wide & (i < block_count - 1))]
    candidates += [(global_ref[0, n], None) for n in range(2)]
    candidates += [(random_ref[0, i, n], None) for n in range(random_ref.shape[2])]
    for block_id, listed in candidates:
        unusable = functools.reduce(jnp.logical_or, [block_id == t for t in ids])
        if listed is not None:
            unusable = unusable | jnp.logical_not(listed)
        ids.append(jnp.where(unusable, i, block_id))
        penalties.append(jnp.where(unusable, jnp.float32(PENALTY), jnp.float32(0.0)))
    return ids, penalties


def sparse_blocks(step, group, global_ref):
    low = jnp.minimum(global_ref[0, 0], global_ref[0, 1])
    high = jnp.maximum(global_ref[0, 0], global_ref[0, 1])
    blocks = []
    for u in range(group):
        n = step * group + u
        i = n + (n >= low).astype(jnp.int32)
        blocks.append(i + (i >= high).astype(jnp.int32))
    return blocks


def load_all(x_hbm, x_ref, sems):
    copies = [pltpu.make_async_copy(x_hbm.at[:, n], x_ref.at[n], sems.at[n]) for n in range(4)]
    for n in (KEY, QUERY, VALUE, D_OUT):
        copies[n].start()
    return copies


def scale_keys(x_ref, ks_ref, gain_k):
    def body(j, carry):
        ks_ref[j] = (x_ref[KEY, j].astype(F32) * gain_k).astype(BF16)
        return carry

    loop(ks_ref.shape[0], body, 0, 8)


def pair(ref, g0, g1):
    return jnp.concatenate([ref[g0], ref[g1]], 0)


def chunk_of(ref, c):
    return ref[pl.ds(c * CHUNK, CHUNK)].reshape(CHUNK * BLOCK, HD)


def main_kernel(
    width_ref, global_ref, random_ref, x_hbm, gain_ref, y_hbm, lse_hbm, terms_ref,
    x_ref, ks_ref, p_ref, dk_ref, y_ref, lse_ref, tq_ref, in_sems, out_sems, lse_sem,
):
    copies = load_all(x_hbm, x_ref, in_sems)
    block_count = ks_ref.shape[0]
    chunks = block_count // CHUNK
    gain_q = gain_ref[0:1, :]
    gain_k = gain_ref[1:2, :]
    g0 = global_ref[0, 0]
    g1 = global_ref[0, 1]
    k_raw, v_ref, q_ref, d_ref = (x_ref.at[n] for n in (KEY, VALUE, QUERY, D_OUT))
    copies[KEY].wait()
    scale_keys(x_ref, ks_ref, gain_k)
    copies[QUERY].wait()

    q_raw = pair(q_ref, g0, g1).astype(F32)
    q_scaled = (q_raw * gain_q).astype(BF16)
    rows = 2 * BLOCK

    def full_scores(c, top):
        scores = dot_nt(q_scaled, chunk_of(ks_ref, c))
        p_ref[c] = scores
        return jnp.maximum(top, lane_fold(jnp.maximum, scores))

    top = loop(chunks, full_scores, jnp.full((rows, BLOCK), -3e38, F32))
    top = jnp.max(top, axis=1, keepdims=True) * SCALE_LOG2

    def full_exp(c, total):
        e = jnp.exp2(p_ref[c] * SCALE_LOG2 - top)
        p_ref[c] = e
        return total + lane_fold(jnp.add, e)

    total = row_sum(loop(chunks, full_exp, jnp.zeros((rows, BLOCK), F32)))
    inverse = 1.0 / total
    lse = jnp.broadcast_to(top + jnp.log(total) * LOG2E, (rows, BLOCK))
    lse_ref[g0] = lse[:BLOCK]
    lse_ref[g1] = lse[BLOCK:]
    copies[VALUE].wait()
    copies[D_OUT].wait()
    d_out = pair(d_ref, g0, g1)

    def full_out(c, acc):
        p = p_ref[c] * inverse
        p_ref[c] = p
        return acc + dot_nn(p.astype(BF16), chunk_of(v_ref, c))

    out = loop(chunks, full_out, jnp.zeros((rows, HD), F32)).astype(BF16)
    y_ref[g0, 0] = out[:BLOCK]
    y_ref[g1, 0] = out[BLOCK:]
    row_dot = row_sum(d_out.astype(F32) * out.astype(F32))

    def full_back(c, acc):
        ds = (p_ref[c] * (dot_nt(d_out, chunk_of(v_ref, c)) - row_dot)).astype(BF16)
        dk_t = dot_tn(q_scaled, ds)
        for n in range(CHUNK):
            dk_ref[c * CHUNK + n] = slot_of(dk_t, n)
        return acc + dot_nn(ds, chunk_of(ks_ref, c))

    dq = loop(chunks, full_back, jnp.zeros((rows, HD), F32)) * SCALE
    dq_b = (dq * gain_q).astype(BF16)
    y_ref[g0, 1] = dq_b[:BLOCK]
    y_ref[g1, 1] = dq_b[BLOCK:]
    terms = dq * q_raw
    tq_ref[...] = terms[:BLOCK] + terms[BLOCK:]

    def step(n, carry):
        blocks = sparse_blocks(n, GROUP, global_ref)
        us = range(GROUP)
        slots = [key_slots(i, width_ref, global_ref, random_ref, block_count) for i in blocks]
        k_slots = [jnp.concatenate([ks_ref[t] for t in slots[u][0]], 0) for u in us]
        v_slots = [jnp.concatenate([v_ref[t] for t in slots[u][0]], 0) for u in us]
        q_raw = [q_ref[i].astype(F32) for i in blocks]
        q_scaled = [(q * gain_q).astype(BF16) for q in q_raw]
        d_out = [d_ref[i] for i in blocks]
        scores = [dot_nt(q_scaled[u], k_slots[u]) for u in us]
        dps = [dot_nt(d_out[u], v_slots[u]) for u in us]
        tops = [
            jnp.max(lane_fold(jnp.maximum, scores[u]), axis=1, keepdims=True) * SCALE_LOG2
            for u in us
        ]
        es = [
            [
                jnp.exp2(slot_of(scores[u], t) * SCALE_LOG2 - (tops[u] + penalty))
                for t, penalty in enumerate(slots[u][1])
            ]
            for u in us
        ]
        totals = [row_sum(functools.reduce(jnp.add, es[u])) for u in us]
        inverses = [1.0 / totals[u] for u in us]
        ps = [[e * inverses[u] for e in es[u]] for u in us]
        p_b = [jnp.concatenate([p.astype(BF16) for p in ps[u]], 1) for u in us]
        outs = [dot_nn(p_b[u], v_slots[u]).astype(BF16) for u in us]
        row_dots = [row_sum(d_out[u].astype(F32) * outs[u].astype(F32)) for u in us]
        ds = [
            jnp.concatenate(
                [
                    (p * (slot_of(dps[u], t) - row_dots[u])).astype(BF16)
                    for t, p in enumerate(ps[u])
                ],
                1,
            )
            for u in us
        ]
        dqs = [dot_nn(ds[u], k_slots[u]) * SCALE for u in us]
        dk_t = [dot_tn(q_scaled[u], ds[u]) for u in us]
        for u in us:
            y_ref[blocks[u], 0] = outs[u]
            y_ref[blocks[u], 1] = (dqs[u] * gain_q).astype(BF16)
            lse_ref[blocks[u]] = jnp.broadcast_to(
                tops[u] + jnp.log(totals[u]) * LOG2E, (BLOCK, BLOCK)
            )
        tq_ref[...] += functools.reduce(jnp.add, [dqs[u] * q_raw[u] for u in us])
        for u in us:
            for t, block_id in enumerate(slots[u][0]):
                dk_ref[block_id] += slot_of(dk_t[u], t)
        return carry

    lax.fori_loop(0, (block_count - 2) // GROUP, step, 0)
    lse_copy = pltpu.make_async_copy(lse_ref, lse_hbm, lse_sem)

    def finish(j, acc):
        dk = dk_ref[j].T * SCALE
        y_ref[j, 2] = (dk * gain_k).astype(BF16)
        return acc + dk * k_raw[j].astype(F32)

    tk = jnp.zeros((BLOCK, HD), F32)
    size = block_count // PARTS
    out_copies = []
    for part in range(PARTS):
        tk = lax.fori_loop(part * size, (part + 1) * size, finish, tk, unroll=True)
        rows = pl.ds(part * size, size)
        out_copies.append(pltpu.make_async_copy(y_ref.at[rows], y_hbm.at[rows], out_sems.at[part]))
        out_copies[-1].start()
    lse_copy.start()
    terms_ref[0:1, :] = jnp.sum(tq_ref[...], axis=0, keepdims=True)
    terms_ref[1:2, :] = jnp.sum(tk, axis=0, keepdims=True)
    for copy in out_copies:
        copy.wait()
    lse_copy.wait()


def values_kernel(
    width_ref, global_ref, random_ref, x_hbm, gain_ref, lse_hbm, y_hbm,
    x_ref, ks_ref, lse_ref, dv_ref, y_ref, in_sems, lse_sem, out_sem,
):
    lse_copy = pltpu.make_async_copy(lse_hbm, lse_ref, lse_sem)
    lse_copy.start()
    copies = [
        pltpu.make_async_copy(x_hbm.at[:, n], x_ref.at[n], in_sems.at[n])
        for n in (KEY, QUERY, D_OUT)
    ]
    for copy in copies:
        copy.start()
    block_count = ks_ref.shape[0]
    chunks = block_count // CHUNK
    gain_q = gain_ref[0:1, :]
    g0 = global_ref[0, 0]
    g1 = global_ref[0, 1]
    q_ref, d_ref = x_ref.at[QUERY], x_ref.at[D_OUT]
    lse_copy.wait()
    for copy in copies:
        copy.wait()
    scale_keys(x_ref, ks_ref, gain_ref[1:2, :])
    q_scaled = (pair(q_ref, g0, g1).astype(F32) * gain_q).astype(BF16)
    lse = jnp.concatenate([pair(lse_ref, g0, g1)] * CHUNK, 1)
    d_out = pair(d_ref, g0, g1)

    def full_values(c, carry):
        scores = dot_nt(q_scaled, chunk_of(ks_ref, c))
        dv_t = dot_tn(d_out, jnp.exp2(scores * SCALE_LOG2 - lse).astype(BF16))
        for n in range(CHUNK):
            dv_ref[c * CHUNK + n] = slot_of(dv_t, n)
        return carry

    loop(chunks, full_values, 0)

    def step(n, carry):
        blocks = sparse_blocks(n, GROUP, global_ref)
        us = range(GROUP)
        slots = [key_slots(i, width_ref, global_ref, random_ref, block_count) for i in blocks]
        k_slots = [jnp.concatenate([ks_ref[t] for t in slots[u][0]], 0) for u in us]
        q_scaled = [(q_ref[i].astype(F32) * gain_q).astype(BF16) for i in blocks]
        scores = [dot_nt(q_scaled[u], k_slots[u]) for u in us]
        dv_t = []
        for u in us:
            lse = lse_ref[blocks[u]]
            p_b = [
                jnp.exp2(slot_of(scores[u], t) * SCALE_LOG2 - (lse + penalty)).astype(BF16)
                for t, penalty in enumerate(slots[u][1])
            ]
            dv_t.append(dot_tn(d_ref[blocks[u]], jnp.concatenate(p_b, 1)))
        for u in us:
            for t, block_id in enumerate(slots[u][0]):
                dv_ref[block_id] += slot_of(dv_t[u], t)
        return carry

    lax.fori_loop(0, (block_count - 2) // GROUP, step, 0)

    def finish(j, carry):
        y_ref[j] = dv_ref[j].T.astype(BF16)
        return carry

    loop(block_count, finish, 0, 8)
    copy = pltpu.make_async_copy(y_ref, y_hbm.at[:, pl.ds(0, BLOCK)], out_sem)
    copy.start()
    copy.wait()


def attend_without_values(widths, global_ids, random_ids, x, gains):
    blocks = x.shape[0]
    return pl.pallas_call(
        main_kernel,
        out_shape=(
            pltpu.HBM((blocks, 3, BLOCK, HD), BF16),
            pltpu.HBM((blocks, BLOCK, BLOCK), F32),
            jax.ShapeDtypeStruct((2, HD), F32),
        ),
        in_specs=[SMEM, SMEM, SMEM, HBM, VMEM],
        out_specs=(HBM, HBM, VMEM),
        scratch_shapes=[
            pltpu.VMEM((4, blocks, BLOCK, HD), BF16),
            pltpu.VMEM((blocks, BLOCK, HD), BF16),
            pltpu.VMEM((blocks // CHUNK, 2 * BLOCK, CHUNK * BLOCK), F32),
            pltpu.VMEM((blocks, HD, BLOCK), F32),
            pltpu.VMEM((blocks, 3, BLOCK, HD), BF16),
            pltpu.VMEM((blocks, BLOCK, BLOCK), F32),
            pltpu.VMEM((BLOCK, HD), F32),
            pltpu.SemaphoreType.DMA((4,)),
            pltpu.SemaphoreType.DMA((PARTS,)),
            pltpu.SemaphoreType.DMA,
        ],
        compiler_params=pltpu.CompilerParams(vmem_limit_bytes=40 * MIB),
        name="attend_without_values",
    )(widths, global_ids, random_ids, *in_hbm(x), gains)


def value_gradients(widths, global_ids, random_ids, x, gains, lse):
    blocks = x.shape[0]
    return pl.pallas_call(
        values_kernel,
        out_shape=pltpu.HBM((blocks, BLOCK + TERM_ROWS, HD), BF16),
        in_specs=[SMEM, SMEM, SMEM, HBM, VMEM, HBM],
        out_specs=HBM,
        scratch_shapes=[
            pltpu.VMEM((4, blocks, BLOCK, HD), BF16),
            pltpu.VMEM((blocks, BLOCK, HD), BF16),
            pltpu.VMEM((blocks, BLOCK, BLOCK), F32),
            pltpu.VMEM((blocks, HD, BLOCK), F32),
            pltpu.VMEM((blocks, BLOCK, HD), BF16),
            pltpu.SemaphoreType.DMA((4,)),
            pltpu.SemaphoreType.DMA,
            pltpu.SemaphoreType.DMA,
        ],
        compiler_params=pltpu.CompilerParams(vmem_limit_bytes=40 * MIB),
        name="value_gradients",
    )(widths, global_ids, random_ids, *in_hbm(x), gains, *in_hbm(lse))


def put_terms_kernel(y_in, total_ref, y_out, rows_ref, sem):
    total = total_ref[...]
    high = total.astype(BF16)
    low = (total - high.astype(F32)).astype(BF16)
    rows = jnp.concatenate([high, low, jnp.zeros((TERM_ROWS - 4, HD), BF16)], 0)
    rows_ref[...] = jnp.broadcast_to(rows[None], rows_ref.shape)
    copy = pltpu.make_async_copy(rows_ref, y_out.at[:, pl.ds(BLOCK, TERM_ROWS)], sem)
    copy.start()
    copy.wait()


def put_terms(y, total):
    return pl.pallas_call(
        put_terms_kernel,
        out_shape=pltpu.HBM(y.shape, y.dtype),
        in_specs=[HBM, VMEM],
        out_specs=HBM,
        scratch_shapes=[
            pltpu.VMEM((y.shape[0], TERM_ROWS, HD), BF16),
            pltpu.SemaphoreType.DMA,
        ],
        input_output_aliases={0: 0},
        name="put_terms",
    )(*in_hbm(y), total)


def split_kernel(q_hbm, k_hbm, v_hbm, d_hbm, x_hbm, in_ref, x_ref, in_sems, out_sems):
    sources = (q_hbm, k_hbm, v_hbm, d_hbm)
    heads = x_ref.shape[0] // PARTS
    width = heads * HD

    def fetch(c, n):
        src = sources[n].at[0, :, pl.ds(c * width, width)]
        return pltpu.make_async_copy(src, in_ref.at[c, n], in_sems.at[c, n])

    def send(c):
        part = pl.ds(c * heads, heads)
        return pltpu.make_async_copy(x_ref.at[part], x_hbm.at[part], out_sems.at[c])

    for c in range(PARTS):
        for n in range(4):
            fetch(c, n).start()
    for c in range(PARTS):
        for n in range(4):
            fetch(c, n).wait()
            for h in range(heads):
                x_ref[c * heads + h, n] = in_ref[c, n, :, h * HD : (h + 1) * HD]
        send(c).start()
    for c in range(PARTS):
        send(c).wait()


def split_heads(arrays):
    _, tokens, channels = arrays[0].shape
    heads = channels // HD
    return pl.pallas_call(
        split_kernel,
        out_shape=pltpu.HBM((heads, 4, tokens, HD), BF16),
        in_specs=[HBM] * 4,
        out_specs=HBM,
        scratch_shapes=[
            pltpu.VMEM((PARTS, 4, tokens, channels // PARTS), BF16),
            pltpu.VMEM((heads, 4, tokens, HD), BF16),
            pltpu.SemaphoreType.DMA((PARTS, 4)),
            pltpu.SemaphoreType.DMA((PARTS,)),
        ],
        compiler_params=pltpu.CompilerParams(vmem_limit_bytes=16 * MIB),
        name="split_heads",
    )(*in_hbm(*arrays))


def join_kernel(z_hbm, a_hbm, b_hbm, c_hbm, in_ref, out_ref, in_sems, out_sems):
    targets = (a_hbm, b_hbm, c_hbm)
    heads = in_ref.shape[0] // PARTS
    width = heads * HD

    def fetch(c):
        part = pl.ds(c * heads, heads)
        return pltpu.make_async_copy(z_hbm.at[part], in_ref.at[part], in_sems.at[c])

    def send(c, n):
        dst = targets[n].at[0, :, pl.ds(c * width, width)]
        return pltpu.make_async_copy(out_ref.at[c, n], dst, out_sems.at[c, n])

    for c in range(PARTS):
        fetch(c).start()
    for c in range(PARTS):
        fetch(c).wait()
        for n in range(3):
            for h in range(heads):
                out_ref[c, n, :, h * HD : (h + 1) * HD] = in_ref[c * heads + h, n]
            send(c, n).start()
    for c in range(PARTS):
        for n in range(3):
            send(c, n).wait()


def join_terms_kernel(place_ref, z_ref, a_hbm, gains_ref, out_ref, out_sems):
    heads = z_ref.shape[0] // PARTS
    width = heads * HD
    copies = []
    for c in range(PARTS):
        for h in range(heads):
            out_ref[c, :, h * HD : (h + 1) * HD] = z_ref[c * heads + h, 0:BLOCK]
        dst = a_hbm.at[0, :, pl.ds(c * width, width)]
        copies.append(pltpu.make_async_copy(out_ref.at[c], dst, out_sems.at[c]))
        copies[-1].start()
    own = gains_ref.shape[1] // HD
    for n in range(own):
        rows = z_ref[place_ref[0] * own + n, BLOCK : BLOCK + TERM_ROWS].astype(F32)
        gains_ref[:, n * HD : (n + 1) * HD] = rows[0:2] + rows[2:4]
    for copy in copies:
        copy.wait()


def join_heads(z):
    heads = z.shape[0]
    return pl.pallas_call(
        join_kernel,
        out_shape=(pltpu.HBM((1, BLOCK, heads * HD), BF16),) * 3,
        in_specs=[HBM],
        out_specs=(HBM,) * 3,
        scratch_shapes=[
            pltpu.VMEM((heads, 3, BLOCK, HD), BF16),
            pltpu.VMEM((PARTS, 3, BLOCK, heads * HD // PARTS), BF16),
            pltpu.SemaphoreType.DMA((PARTS,)),
            pltpu.SemaphoreType.DMA((PARTS, 3)),
        ],
        compiler_params=pltpu.CompilerParams(vmem_limit_bytes=16 * MIB),
        name="join_heads",
    )(*in_hbm(z))


def join_heads_terms(place, z, own):
    heads = z.shape[0]
    return pl.pallas_call(
        join_terms_kernel,
        out_shape=(
            pltpu.HBM((1, BLOCK, heads * HD), BF16),
            jax.ShapeDtypeStruct((2, own * HD), F32),
        ),
        in_specs=[SMEM, VMEM],
        out_specs=(HBM, VMEM),
        scratch_shapes=[
            pltpu.VMEM((PARTS, BLOCK, heads * HD // PARTS), BF16),
            pltpu.SemaphoreType.DMA((PARTS,)),
        ],
        compiler_params=pltpu.CompilerParams(vmem_limit_bytes=16 * MIB),
        name="join_heads_terms",
    )(place, z)


def exchange(x):
    return lax.all_to_all(x, "ctx", split_axis=0, concat_axis=0, tiled=True)


def sum_over_sequences(terms):
    count = lax.axis_size("dp")
    stride = 1
    while stride < count:
        pairs = [(n, n ^ stride) for n in range(count)]
        terms = terms + lax.ppermute(terms, "dp", pairs)
        stride *= 2
    return terms


def on_device(queries, keys, values, d_out, gains, window_widths, global_blocks, random_blocks):
    x = exchange(split_heads((queries, keys, values, d_out)))
    all_gains = lax.all_gather(gains, "dp", axis=1, tiled=True)
    own_gains = lax.dynamic_slice_in_dim(all_gains, lax.axis_index("ctx") * HD, HD, 1)
    tables = (window_widths, global_blocks, random_blocks)
    y, lse, terms = attend_without_values(*tables, x, own_gains)
    returned = exchange(y)
    d_values = value_gradients(*tables, x, own_gains, lse)
    d_values = put_terms(d_values, sum_over_sequences(terms))
    d_values, returned = lax.optimization_barrier((d_values, returned))
    out, d_queries, d_keys = join_heads(returned)
    place = lax.axis_index("dp").reshape(1)
    d_values, d_gains = join_heads_terms(place, exchange(d_values), gains.shape[1] // HD)
    return (out, d_queries, d_keys, d_values, d_gains)


def solution(mesh):
    tokens = P("dp", "ctx", None)
    return jax.shard_map(
        on_device,
        mesh=mesh,
        in_specs=(
            tokens, tokens, tokens, tokens,
            P(None, "dp"), P("ctx"), P("dp", None), P("dp", None, None),
        ),
        out_specs=(tokens, tokens, tokens, tokens, P(None, "dp")),
        check_vma=False,
    )
```

```python
import functools
import math

import jax
import jax.numpy as jnp
from jax import lax
from jax.experimental import pallas as pl
from jax.experimental.pallas import tpu as pltpu
from jax.sharding import PartitionSpec as P

HD = 128
BLOCK = 128
SCALE = 1.0 / math.sqrt(HD)
LOG2E = math.log2(math.e)
SCALE_LOG2 = SCALE * LOG2E
PENALTY = 1e30
CHUNK = 8
GROUP = 10
PARTS = 4
TERM_ROWS = 8
MIB = 1024 * 1024
F32 = jnp.float32
BF16 = jnp.bfloat16
HBM = pl.BlockSpec(memory_space=pltpu.HBM)
VMEM = pl.BlockSpec(memory_space=pltpu.VMEM)
SMEM = pl.BlockSpec(memory_space=pltpu.SMEM)
QUERY, KEY, VALUE, D_OUT = range(4)


def in_hbm(*arrays):
    return [pltpu.with_memory_space_constraint(a, pltpu.HBM) for a in arrays]


def dot_nn(a, b):
    return lax.dot_general(a, b, (((1,), (0,)), ((), ())), preferred_element_type=F32)


def dot_nt(a, b):
    return lax.dot_general(a, b, (((1,), (1,)), ((), ())), preferred_element_type=F32)


def dot_tn(a, b):
    return lax.dot_general(a, b, (((0,), (0,)), ((), ())), preferred_element_type=F32)


def slot_of(wide, t):
    return wide[:, t * BLOCK : (t + 1) * BLOCK]


def lane_fold(combine, wide):
    return functools.reduce(combine, [slot_of(wide, t) for t in range(wide.shape[1] // BLOCK)])


def row_sum(a):
    return jnp.sum(a, axis=1, keepdims=True)


def loop(count, body, start, unroll=True):
    return lax.fori_loop(0, count, body, start, unroll=unroll)


def key_slots(i, width_ref, global_ref, random_ref, block_count):
    wide = width_ref[0] >= 1
    ids = [i]
    penalties = [jnp.float32(0.0)]
    candidates = [(i - 1, wide & (i > 0)), (i + 1, wide & (i < block_count - 1))]
    candidates += [(global_ref[0, n], None) for n in range(2)]
    candidates += [(random_ref[0, i, n], None) for n in range(random_ref.shape[2])]
    for block_id, listed in candidates:
        unusable = functools.reduce(jnp.logical_or, [block_id == t for t in ids])
        if listed is not None:
            unusable = unusable | jnp.logical_not(listed)
        ids.append(jnp.where(unusable, i, block_id))
        penalties.append(jnp.where(unusable, jnp.float32(PENALTY), jnp.float32(0.0)))
    return ids, penalties


def split_slots(i, width_ref, global_ref, random_ref, block_count):
    ids, penalties = key_slots(i, width_ref, global_ref, random_ref, block_count)
    own = [0, 1, 2] + list(range(5, len(ids)))
    return [ids[t] for t in own], [penalties[t] for t in own], penalties[3:5]


def sparse_blocks(step, group, global_ref):
    low = jnp.minimum(global_ref[0, 0], global_ref[0, 1])
    high = jnp.maximum(global_ref[0, 0], global_ref[0, 1])
    blocks = []
    for u in range(group):
        n = step * group + u
        i = n + (n >= low).astype(jnp.int32)
        blocks.append(i + (i >= high).astype(jnp.int32))
    return blocks


def load_all(x_hbm, x_ref, sems):
    copies = [pltpu.make_async_copy(x_hbm.at[:, n], x_ref.at[n], sems.at[n]) for n in range(4)]
    for n in (KEY, QUERY, VALUE, D_OUT):
        copies[n].start()
    return copies


def scale_keys(x_ref, ks_ref, gain_k):
    def body(j, carry):
        ks_ref[j] = (x_ref[KEY, j].astype(F32) * gain_k).astype(BF16)
        return carry

    loop(ks_ref.shape[0], body, 0, 8)


def pair(ref, g0, g1):
    return jnp.concatenate([ref[g0], ref[g1]], 0)


def chunk_of(ref, c):
    return ref[pl.ds(c * CHUNK, CHUNK)].reshape(CHUNK * BLOCK, HD)


def main_kernel(
    width_ref, global_ref, random_ref, x_hbm, gain_ref, y_hbm, lse_hbm, terms_ref,
    x_ref, ks_ref, p_ref, dk_ref, y_ref, lse_ref, tq_ref, in_sems, out_sems, row_sem, lse_sem,
):
    copies = load_all(x_hbm, x_ref, in_sems)
    block_count = ks_ref.shape[0]
    chunks = block_count // CHUNK
    gain_q = gain_ref[0:1, :]
    gain_k = gain_ref[1:2, :]
    g0 = global_ref[0, 0]
    g1 = global_ref[0, 1]
    k_raw, v_ref, q_ref, d_ref = (x_ref.at[n] for n in (KEY, VALUE, QUERY, D_OUT))
    copies[KEY].wait()
    scale_keys(x_ref, ks_ref, gain_k)
    copies[QUERY].wait()

    q_raw = pair(q_ref, g0, g1).astype(F32)
    q_scaled = (q_raw * gain_q).astype(BF16)
    rows = 2 * BLOCK

    def full_scores(c, top):
        scores = dot_nt(q_scaled, chunk_of(ks_ref, c))
        p_ref[c] = scores
        return jnp.maximum(top, lane_fold(jnp.maximum, scores))

    top = loop(chunks, full_scores, jnp.full((rows, BLOCK), -3e38, F32))
    top = jnp.max(top, axis=1, keepdims=True) * SCALE_LOG2

    def full_exp(c, total):
        e = jnp.exp2(p_ref[c] * SCALE_LOG2 - top)
        p_ref[c] = e
        return total + lane_fold(jnp.add, e)

    total = row_sum(loop(chunks, full_exp, jnp.zeros((rows, BLOCK), F32)))
    inverse = 1.0 / total
    lse = jnp.broadcast_to(top + jnp.log(total) * LOG2E, (rows, BLOCK))
    lse_ref[g0] = lse[:BLOCK]
    lse_ref[g1] = lse[BLOCK:]
    copies[VALUE].wait()
    copies[D_OUT].wait()
    d_out = pair(d_ref, g0, g1)

    def full_out(c, acc):
        p = p_ref[c] * inverse
        p_ref[c] = p
        return acc + dot_nn(p.astype(BF16), chunk_of(v_ref, c))

    out = loop(chunks, full_out, jnp.zeros((rows, HD), F32)).astype(BF16)
    y_ref[g0, 0] = out[:BLOCK]
    y_ref[g1, 0] = out[BLOCK:]
    row_dot = row_sum(d_out.astype(F32) * out.astype(F32))

    def full_back(c, acc):
        ds = (p_ref[c] * (dot_nt(d_out, chunk_of(v_ref, c)) - row_dot)).astype(BF16)
        dk_t = dot_tn(q_scaled, ds)
        for n in range(CHUNK):
            dk_ref[c * CHUNK + n] = slot_of(dk_t, n)
        return acc + dot_nn(ds, chunk_of(ks_ref, c))

    dq = loop(chunks, full_back, jnp.zeros((rows, HD), F32)) * SCALE
    dq_b = (dq * gain_q).astype(BF16)
    y_ref[g0, 1] = dq_b[:BLOCK]
    y_ref[g1, 1] = dq_b[BLOCK:]
    terms = dq * q_raw
    tq_ref[...] = terms[:BLOCK] + terms[BLOCK:]

    def send_block(i):
        pltpu.make_async_copy(y_ref.at[i, pl.ds(0, 2)], y_hbm.at[i, pl.ds(0, 2)], row_sem).start()
        pltpu.make_async_copy(lse_ref.at[i], lse_hbm.at[i], lse_sem).start()

    send_block(g0)
    send_block(g1)

    def step(n, carry):
        blocks = sparse_blocks(n, GROUP, global_ref)
        us = range(GROUP)
        slots = [split_slots(i, width_ref, global_ref, random_ref, block_count) for i in blocks]
        k_slots = [jnp.concatenate([ks_ref[t] for t in slots[u][0]], 0) for u in us]
        v_slots = [jnp.concatenate([v_ref[t] for t in slots[u][0]], 0) for u in us]
        k_global = pair(ks_ref, g0, g1)
        v_global = pair(v_ref, g0, g1)

        def rows_of(stacked, u):
            return stacked[u * BLOCK : (u + 1) * BLOCK]

        q_raw = [q_ref[i].astype(F32) for i in blocks]
        q_scaled = [(q * gain_q).astype(BF16) for q in q_raw]
        q_all = jnp.concatenate(q_scaled, 0)
        d_out = [d_ref[i] for i in blocks]
        scores = [dot_nt(q_scaled[u], k_slots[u]) for u in us]
        scores_global = dot_nt(q_all, k_global)
        dps = [dot_nt(d_out[u], v_slots[u]) for u in us]
        dps_global = dot_nt(jnp.concatenate(d_out, 0), v_global)

        def tiles(own, shared, u):
            own_tiles = [slot_of(own[u], t) for t in range(own[u].shape[1] // BLOCK)]
            return own_tiles + [slot_of(rows_of(shared, u), t) for t in range(2)]

        s_tiles = [tiles(scores, scores_global, u) for u in us]
        d_tiles = [tiles(dps, dps_global, u) for u in us]
        tops = [
            jnp.max(functools.reduce(jnp.maximum, s_tiles[u]), axis=1, keepdims=True) * SCALE_LOG2
            for u in us
        ]
        es = [
            [
                jnp.exp2(tile * SCALE_LOG2 - (tops[u] + penalty))
                for tile, penalty in zip(s_tiles[u], slots[u][1] + slots[u][2])
            ]
            for u in us
        ]
        totals = [row_sum(functools.reduce(jnp.add, es[u])) for u in us]
        inverses = [1.0 / totals[u] for u in us]
        ps = [[e * inverses[u] for e in es[u]] for u in us]
        p_b = [[p.astype(BF16) for p in ps[u]] for u in us]
        out_global = dot_nn(
            jnp.concatenate([jnp.concatenate(p_b[u][-2:], 1) for u in us], 0), v_global
        )
        outs = [
            (dot_nn(jnp.concatenate(p_b[u][:-2], 1), v_slots[u]) + rows_of(out_global, u)).astype(BF16)
            for u in us
        ]
        row_dots = [row_sum(d_out[u].astype(F32) * outs[u].astype(F32)) for u in us]
        ds = [
            [(p * (tile - row_dots[u])).astype(BF16) for p, tile in zip(ps[u], d_tiles[u])]
            for u in us
        ]
        ds_own = [jnp.concatenate(ds[u][:-2], 1) for u in us]
        ds_global = jnp.concatenate([jnp.concatenate(ds[u][-2:], 1) for u in us], 0)
        dq_global = dot_nn(ds_global, k_global)
        dqs = [(dot_nn(ds_own[u], k_slots[u]) + rows_of(dq_global, u)) * SCALE for u in us]
        dk_t = [dot_tn(q_scaled[u], ds_own[u]) for u in us]
        dk_global = dot_tn(q_all, ds_global)
        for u in us:
            y_ref[blocks[u], 0] = outs[u]
            y_ref[blocks[u], 1] = (dqs[u] * gain_q).astype(BF16)
            lse_ref[blocks[u]] = jnp.broadcast_to(
                tops[u] + jnp.log(totals[u]) * LOG2E, (BLOCK, BLOCK)
            )
            send_block(blocks[u])
        tq_ref[...] += functools.reduce(jnp.add, [dqs[u] * q_raw[u] for u in us])
        for u in us:
            for t, block_id in enumerate(slots[u][0]):
                dk_ref[block_id] += slot_of(dk_t[u], t)
        dk_ref[g0] += slot_of(dk_global, 0)
        dk_ref[g1] += slot_of(dk_global, 1)
        return carry

    lax.fori_loop(0, (block_count - 2) // GROUP, step, 0)

    def finish(j, acc):
        dk = dk_ref[j].T * SCALE
        y_ref[j, 2] = (dk * gain_k).astype(BF16)
        return acc + dk * k_raw[j].astype(F32)

    tk = jnp.zeros((BLOCK, HD), F32)
    size = block_count // PARTS
    out_copies = []
    for part in range(PARTS):
        tk = lax.fori_loop(part * size, (part + 1) * size, finish, tk, unroll=True)
        rows = pl.ds(part * size, size)
        src, dst = y_ref.at[rows, 2], y_hbm.at[rows, 2]
        out_copies.append(pltpu.make_async_copy(src, dst, out_sems.at[part]))
        out_copies[-1].start()
    terms_ref[0:1, :] = jnp.sum(tq_ref[...], axis=0, keepdims=True)
    terms_ref[1:2, :] = jnp.sum(tk, axis=0, keepdims=True)
    for copy in out_copies:
        copy.wait()
    first = pl.ds(0, 2)
    pltpu.make_async_copy(y_ref.at[:, first], y_hbm.at[:, first], row_sem).wait()
    pltpu.make_async_copy(lse_ref, lse_hbm, lse_sem).wait()


def values_kernel(
    width_ref, global_ref, random_ref, x_hbm, gain_ref, lse_hbm, y_hbm,
    x_ref, ks_ref, lse_ref, dv_ref, y_ref, in_sems, lse_sem, out_sem,
):
    lse_copy = pltpu.make_async_copy(lse_hbm, lse_ref, lse_sem)
    lse_copy.start()
    copies = [
        pltpu.make_async_copy(x_hbm.at[:, n], x_ref.at[n], in_sems.at[n])
        for n in (KEY, QUERY, D_OUT)
    ]
    for copy in copies:
        copy.start()
    block_count = ks_ref.shape[0]
    chunks = block_count // CHUNK
    gain_q = gain_ref[0:1, :]
    g0 = global_ref[0, 0]
    g1 = global_ref[0, 1]
    q_ref, d_ref = x_ref.at[QUERY], x_ref.at[D_OUT]
    lse_copy.wait()
    for copy in copies:
        copy.wait()
    scale_keys(x_ref, ks_ref, gain_ref[1:2, :])
    q_scaled = (pair(q_ref, g0, g1).astype(F32) * gain_q).astype(BF16)
    lse = jnp.concatenate([pair(lse_ref, g0, g1)] * CHUNK, 1)
    d_out = pair(d_ref, g0, g1)

    def full_values(c, carry):
        scores = dot_nt(q_scaled, chunk_of(ks_ref, c))
        dv_t = dot_tn(d_out, jnp.exp2(scores * SCALE_LOG2 - lse).astype(BF16))
        for n in range(CHUNK):
            dv_ref[c * CHUNK + n] = slot_of(dv_t, n)
        return carry

    loop(chunks, full_values, 0)

    def step(n, carry):
        blocks = sparse_blocks(n, GROUP, global_ref)
        us = range(GROUP)
        slots = [key_slots(i, width_ref, global_ref, random_ref, block_count) for i in blocks]
        k_slots = [jnp.concatenate([ks_ref[t] for t in slots[u][0]], 0) for u in us]
        q_scaled = [(q_ref[i].astype(F32) * gain_q).astype(BF16) for i in blocks]
        scores = [dot_nt(q_scaled[u], k_slots[u]) for u in us]
        dv_t = []
        for u in us:
            lse = lse_ref[blocks[u]]
            p_b = [
                jnp.exp2(slot_of(scores[u], t) * SCALE_LOG2 - (lse + penalty)).astype(BF16)
                for t, penalty in enumerate(slots[u][1])
            ]
            dv_t.append(dot_tn(d_ref[blocks[u]], jnp.concatenate(p_b, 1)))
        for u in us:
            for t, block_id in enumerate(slots[u][0]):
                dv_ref[block_id] += slot_of(dv_t[u], t)
        return carry

    lax.fori_loop(0, (block_count - 2) // GROUP, step, 0)

    def finish(j, carry):
        y_ref[j] = dv_ref[j].T.astype(BF16)
        return carry

    loop(block_count, finish, 0, 8)
    copy = pltpu.make_async_copy(y_ref, y_hbm.at[:, pl.ds(0, BLOCK)], out_sem)
    copy.start()
    copy.wait()


def attend_without_values(widths, global_ids, random_ids, x, gains):
    blocks = x.shape[0]
    return pl.pallas_call(
        main_kernel,
        out_shape=(
            pltpu.HBM((blocks, 3, BLOCK, HD), BF16),
            pltpu.HBM((blocks, BLOCK, BLOCK), F32),
            jax.ShapeDtypeStruct((2, HD), F32),
        ),
        in_specs=[SMEM, SMEM, SMEM, HBM, VMEM],
        out_specs=(HBM, HBM, VMEM),
        scratch_shapes=[
            pltpu.VMEM((4, blocks, BLOCK, HD), BF16),
            pltpu.VMEM((blocks, BLOCK, HD), BF16),
            pltpu.VMEM((blocks // CHUNK, 2 * BLOCK, CHUNK * BLOCK), F32),
            pltpu.VMEM((blocks, HD, BLOCK), F32),
            pltpu.VMEM((blocks, 3, BLOCK, HD), BF16),
            pltpu.VMEM((blocks, BLOCK, BLOCK), F32),
            pltpu.VMEM((BLOCK, HD), F32),
            pltpu.SemaphoreType.DMA((4,)),
            pltpu.SemaphoreType.DMA((PARTS,)),
            pltpu.SemaphoreType.DMA,
            pltpu.SemaphoreType.DMA,
        ],
        compiler_params=pltpu.CompilerParams(vmem_limit_bytes=40 * MIB),
        name="attend_without_values",
    )(widths, global_ids, random_ids, *in_hbm(x), gains)


def value_gradients(widths, global_ids, random_ids, x, gains, lse):
    blocks = x.shape[0]
    return pl.pallas_call(
        values_kernel,
        out_shape=pltpu.HBM((blocks, BLOCK + TERM_ROWS, HD), BF16),
        in_specs=[SMEM, SMEM, SMEM, HBM, VMEM, HBM],
        out_specs=HBM,
        scratch_shapes=[
            pltpu.VMEM((4, blocks, BLOCK, HD), BF16),
            pltpu.VMEM((blocks, BLOCK, HD), BF16),
            pltpu.VMEM((blocks, BLOCK, BLOCK), F32),
            pltpu.VMEM((blocks, HD, BLOCK), F32),
            pltpu.VMEM((blocks, BLOCK, HD), BF16),
            pltpu.SemaphoreType.DMA((4,)),
            pltpu.SemaphoreType.DMA,
            pltpu.SemaphoreType.DMA,
        ],
        compiler_params=pltpu.CompilerParams(vmem_limit_bytes=62 * MIB),
        name="value_gradients",
    )(widths, global_ids, random_ids, *in_hbm(x), gains, *in_hbm(lse))


def put_terms_kernel(y_in, total_ref, y_out, rows_ref, sem):
    total = total_ref[...]
    high = total.astype(BF16)
    low = (total - high.astype(F32)).astype(BF16)
    rows = jnp.concatenate([high, low, jnp.zeros((TERM_ROWS - 4, HD), BF16)], 0)
    rows_ref[...] = jnp.broadcast_to(rows[None], rows_ref.shape)
    copy = pltpu.make_async_copy(rows_ref, y_out.at[:, pl.ds(BLOCK, TERM_ROWS)], sem)
    copy.start()
    copy.wait()


def put_terms(y, total):
    return pl.pallas_call(
        put_terms_kernel,
        out_shape=pltpu.HBM(y.shape, y.dtype),
        in_specs=[HBM, VMEM],
        out_specs=HBM,
        scratch_shapes=[
            pltpu.VMEM((y.shape[0], TERM_ROWS, HD), BF16),
            pltpu.SemaphoreType.DMA,
        ],
        input_output_aliases={0: 0},
        name="put_terms",
    )(*in_hbm(y), total)


def split_kernel(q_hbm, k_hbm, v_hbm, d_hbm, x_hbm, in_ref, x_ref, in_sems, out_sems):
    sources = (q_hbm, k_hbm, v_hbm, d_hbm)
    heads = x_ref.shape[0] // PARTS
    width = heads * HD

    def fetch(c, n):
        src = sources[n].at[0, :, pl.ds(c * width, width)]
        return pltpu.make_async_copy(src, in_ref.at[c, n], in_sems.at[c, n])

    def send(c):
        part = pl.ds(c * heads, heads)
        return pltpu.make_async_copy(x_ref.at[part], x_hbm.at[part], out_sems.at[c])

    for c in range(PARTS):
        for n in range(4):
            fetch(c, n).start()
    for c in range(PARTS):
        for n in range(4):
            fetch(c, n).wait()
            for h in range(heads):
                x_ref[c * heads + h, n] = in_ref[c, n, :, h * HD : (h + 1) * HD]
        send(c).start()
    for c in range(PARTS):
        send(c).wait()


def split_heads(arrays):
    _, tokens, channels = arrays[0].shape
    heads = channels // HD
    return pl.pallas_call(
        split_kernel,
        out_shape=pltpu.HBM((heads, 4, tokens, HD), BF16),
        in_specs=[HBM] * 4,
        out_specs=HBM,
        scratch_shapes=[
            pltpu.VMEM((PARTS, 4, tokens, channels // PARTS), BF16),
            pltpu.VMEM((heads, 4, tokens, HD), BF16),
            pltpu.SemaphoreType.DMA((PARTS, 4)),
            pltpu.SemaphoreType.DMA((PARTS,)),
        ],
        compiler_params=pltpu.CompilerParams(vmem_limit_bytes=16 * MIB),
        name="split_heads",
    )(*in_hbm(*arrays))


def join_kernel(z_hbm, a_hbm, b_hbm, c_hbm, in_ref, out_ref, in_sems, out_sems):
    targets = (a_hbm, b_hbm, c_hbm)
    heads = in_ref.shape[0] // PARTS
    width = heads * HD

    def fetch(c):
        part = pl.ds(c * heads, heads)
        return pltpu.make_async_copy(z_hbm.at[part], in_ref.at[part], in_sems.at[c])

    def send(c, n):
        dst = targets[n].at[0, :, pl.ds(c * width, width)]
        return pltpu.make_async_copy(out_ref.at[c, n], dst, out_sems.at[c, n])

    for c in range(PARTS):
        fetch(c).start()
    for c in range(PARTS):
        fetch(c).wait()
        for n in range(3):
            for h in range(heads):
                out_ref[c, n, :, h * HD : (h + 1) * HD] = in_ref[c * heads + h, n]
            send(c, n).start()
    for c in range(PARTS):
        for n in range(3):
            send(c, n).wait()


def join_terms_kernel(place_ref, z_ref, a_hbm, gains_ref, out_ref, out_sems):
    heads = z_ref.shape[0] // PARTS
    width = heads * HD
    copies = []
    for c in range(PARTS):
        for h in range(heads):
            out_ref[c, :, h * HD : (h + 1) * HD] = z_ref[c * heads + h, 0:BLOCK]
        dst = a_hbm.at[0, :, pl.ds(c * width, width)]
        copies.append(pltpu.make_async_copy(out_ref.at[c], dst, out_sems.at[c]))
        copies[-1].start()
    own = gains_ref.shape[1] // HD
    for n in range(own):
        rows = z_ref[place_ref[0] * own + n, BLOCK : BLOCK + TERM_ROWS].astype(F32)
        gains_ref[:, n * HD : (n + 1) * HD] = rows[0:2] + rows[2:4]
    for copy in copies:
        copy.wait()


def join_heads(z):
    heads = z.shape[0]
    return pl.pallas_call(
        join_kernel,
        out_shape=(pltpu.HBM((1, BLOCK, heads * HD), BF16),) * 3,
        in_specs=[HBM],
        out_specs=(HBM,) * 3,
        scratch_shapes=[
            pltpu.VMEM((heads, 3, BLOCK, HD), BF16),
            pltpu.VMEM((PARTS, 3, BLOCK, heads * HD // PARTS), BF16),
            pltpu.SemaphoreType.DMA((PARTS,)),
            pltpu.SemaphoreType.DMA((PARTS, 3)),
        ],
        compiler_params=pltpu.CompilerParams(vmem_limit_bytes=16 * MIB),
        name="join_heads",
    )(*in_hbm(z))


def join_heads_terms(place, z, own):
    heads = z.shape[0]
    return pl.pallas_call(
        join_terms_kernel,
        out_shape=(
            pltpu.HBM((1, BLOCK, heads * HD), BF16),
            jax.ShapeDtypeStruct((2, own * HD), F32),
        ),
        in_specs=[SMEM, VMEM],
        out_specs=(HBM, VMEM),
        scratch_shapes=[
            pltpu.VMEM((PARTS, BLOCK, heads * HD // PARTS), BF16),
            pltpu.SemaphoreType.DMA((PARTS,)),
        ],
        compiler_params=pltpu.CompilerParams(vmem_limit_bytes=16 * MIB),
        name="join_heads_terms",
    )(place, z)


def exchange(x):
    return lax.all_to_all(x, "ctx", split_axis=0, concat_axis=0, tiled=True)


def sum_over_sequences(terms):
    count = lax.axis_size("dp")
    stride = 1
    while stride < count:
        pairs = [(n, n ^ stride) for n in range(count)]
        terms = terms + lax.ppermute(terms, "dp", pairs)
        stride *= 2
    return terms


def on_device(queries, keys, values, d_out, gains, window_widths, global_blocks, random_blocks):
    x = exchange(split_heads((queries, keys, values, d_out)))
    all_gains = lax.all_gather(gains, "dp", axis=1, tiled=True)
    own_gains = lax.dynamic_slice_in_dim(all_gains, lax.axis_index("ctx") * HD, HD, 1)
    tables = (window_widths, global_blocks, random_blocks)
    y, lse, terms = attend_without_values(*tables, x, own_gains)
    returned = exchange(y)
    d_values = value_gradients(*tables, x, own_gains, lse)
    d_values = put_terms(d_values, sum_over_sequences(terms))
    d_values, returned = lax.optimization_barrier((d_values, returned))
    out, d_queries, d_keys = join_heads(returned)
    place = lax.axis_index("dp").reshape(1)
    d_values, d_gains = join_heads_terms(place, exchange(d_values), gains.shape[1] // HD)
    return (out, d_queries, d_keys, d_values, d_gains)


def solution(mesh):
    tokens = P("dp", "ctx", None)
    return jax.shard_map(
        on_device,
        mesh=mesh,
        in_specs=(
            tokens, tokens, tokens, tokens,
            P(None, "dp"), P("ctx"), P("dp", None), P("dp", None, None),
        ),
        out_specs=(tokens, tokens, tokens, tokens, P(None, "dp")),
        check_vma=False,
    )
```

```python
import functools
import math

import jax
import jax.numpy as jnp
from jax import lax
from jax.experimental import pallas as pl
from jax.experimental.pallas import tpu as pltpu
from jax.sharding import PartitionSpec as P

HD = 128
BLOCK = 128
SCALE = 1.0 / math.sqrt(HD)
LOG2E = math.log2(math.e)
SCALE_LOG2 = SCALE * LOG2E
PENALTY = 1e30
CHUNK = 32
GROUP = 10
PARTS = 4
TERM_ROWS = 8
MIB = 1024 * 1024
F32 = jnp.float32
BF16 = jnp.bfloat16
HBM = pl.BlockSpec(memory_space=pltpu.HBM)
VMEM = pl.BlockSpec(memory_space=pltpu.VMEM)
SMEM = pl.BlockSpec(memory_space=pltpu.SMEM)
QUERY, KEY, VALUE, D_OUT = range(4)


def in_hbm(*arrays):
    return [pltpu.with_memory_space_constraint(a, pltpu.HBM) for a in arrays]


def dot_nn(a, b):
    return lax.dot_general(a, b, (((1,), (0,)), ((), ())), preferred_element_type=F32)


def dot_nt(a, b):
    return lax.dot_general(a, b, (((1,), (1,)), ((), ())), preferred_element_type=F32)


def dot_tn(a, b):
    return lax.dot_general(a, b, (((0,), (0,)), ((), ())), preferred_element_type=F32)


def slot_of(wide, t):
    return wide[:, t * BLOCK : (t + 1) * BLOCK]


def lane_fold(combine, wide):
    return functools.reduce(combine, [slot_of(wide, t) for t in range(wide.shape[1] // BLOCK)])


def row_sum(a):
    return jnp.sum(a, axis=1, keepdims=True)


def loop(count, body, start, unroll=True):
    return lax.fori_loop(0, count, body, start, unroll=unroll)


def key_slots(i, width_ref, global_ref, random_ref, block_count):
    wide = width_ref[0] >= 1
    ids = [i]
    penalties = [jnp.float32(0.0)]
    candidates = [(i - 1, wide & (i > 0)), (i + 1, wide & (i < block_count - 1))]
    candidates += [(global_ref[0, n], None) for n in range(2)]
    candidates += [(random_ref[0, i, n], None) for n in range(random_ref.shape[2])]
    for block_id, listed in candidates:
        unusable = functools.reduce(jnp.logical_or, [block_id == t for t in ids])
        if listed is not None:
            unusable = unusable | jnp.logical_not(listed)
        ids.append(jnp.where(unusable, i, block_id))
        penalties.append(jnp.where(unusable, jnp.float32(PENALTY), jnp.float32(0.0)))
    return ids, penalties


def split_slots(i, width_ref, global_ref, random_ref, block_count):
    ids, penalties = key_slots(i, width_ref, global_ref, random_ref, block_count)
    own = [0, 1, 2] + list(range(5, len(ids)))
    return [ids[t] for t in own], [penalties[t] for t in own], penalties[3:5]


def sparse_blocks(step, group, global_ref):
    low = jnp.minimum(global_ref[0, 0], global_ref[0, 1])
    high = jnp.maximum(global_ref[0, 0], global_ref[0, 1])
    blocks = []
    for u in range(group):
        n = step * group + u
        i = n + (n >= low).astype(jnp.int32)
        blocks.append(i + (i >= high).astype(jnp.int32))
    return blocks


def load_all(x_hbm, x_ref, sems):
    copies = [pltpu.make_async_copy(x_hbm.at[:, n], x_ref.at[n], sems.at[n]) for n in range(4)]
    for n in (KEY, QUERY, VALUE, D_OUT):
        copies[n].start()
    return copies


def scale_keys(x_ref, ks_ref, gain_k):
    def body(j, carry):
        ks_ref[j] = (x_ref[KEY, j].astype(F32) * gain_k).astype(BF16)
        return carry

    loop(ks_ref.shape[0], body, 0, 8)


def pair(ref, g0, g1):
    return jnp.concatenate([ref[g0], ref[g1]], 0)


def chunk_of(ref, c):
    return ref[pl.ds(c * CHUNK, CHUNK)].reshape(CHUNK * BLOCK, HD)


def main_kernel(
    width_ref, global_ref, random_ref, x_hbm, gain_ref, y_hbm, lse_hbm, terms_ref,
    x_ref, ks_ref, p_ref, dk_ref, y_ref, lse_ref, tq_ref, in_sems, out_sems, row_sem, lse_sem,
):
    copies = load_all(x_hbm, x_ref, in_sems)
    block_count = ks_ref.shape[0]
    chunks = block_count // CHUNK
    gain_q = gain_ref[0:1, :]
    gain_k = gain_ref[1:2, :]
    g0 = global_ref[0, 0]
    g1 = global_ref[0, 1]
    k_raw, v_ref, q_ref, d_ref = (x_ref.at[n] for n in (KEY, VALUE, QUERY, D_OUT))
    copies[KEY].wait()
    scale_keys(x_ref, ks_ref, gain_k)
    copies[QUERY].wait()

    q_raw = pair(q_ref, g0, g1).astype(F32)
    q_scaled = (q_raw * gain_q).astype(BF16)
    rows = 2 * BLOCK

    def full_scores(c, top):
        scores = dot_nt(q_scaled, chunk_of(ks_ref, c))
        p_ref[c] = scores
        return jnp.maximum(top, lane_fold(jnp.maximum, scores))

    top = loop(chunks, full_scores, jnp.full((rows, BLOCK), -3e38, F32))
    top = jnp.max(top, axis=1, keepdims=True) * SCALE_LOG2

    def full_exp(c, total):
        e = jnp.exp2(p_ref[c] * SCALE_LOG2 - top)
        p_ref[c] = e
        return total + lane_fold(jnp.add, e)

    total = row_sum(loop(chunks, full_exp, jnp.zeros((rows, BLOCK), F32)))
    inverse = 1.0 / total
    lse = jnp.broadcast_to(top + jnp.log(total) * LOG2E, (rows, BLOCK))
    lse_ref[g0] = lse[:BLOCK]
    lse_ref[g1] = lse[BLOCK:]
    copies[VALUE].wait()
    copies[D_OUT].wait()
    d_out = pair(d_ref, g0, g1)

    def full_out(c, acc):
        p = p_ref[c] * inverse
        p_ref[c] = p
        return acc + dot_nn(p.astype(BF16), chunk_of(v_ref, c))

    out = loop(chunks, full_out, jnp.zeros((rows, HD), F32)).astype(BF16)
    y_ref[g0, 0] = out[:BLOCK]
    y_ref[g1, 0] = out[BLOCK:]
    row_dot = row_sum(d_out.astype(F32) * out.astype(F32))

    def full_back(c, acc):
        ds = (p_ref[c] * (dot_nt(d_out, chunk_of(v_ref, c)) - row_dot)).astype(BF16)
        dk_t = dot_tn(q_scaled, ds)
        for n in range(CHUNK):
            dk_ref[c * CHUNK + n] = slot_of(dk_t, n)
        return acc + dot_nn(ds, chunk_of(ks_ref, c))

    dq = loop(chunks, full_back, jnp.zeros((rows, HD), F32)) * SCALE
    dq_b = (dq * gain_q).astype(BF16)
    y_ref[g0, 1] = dq_b[:BLOCK]
    y_ref[g1, 1] = dq_b[BLOCK:]
    terms = dq * q_raw
    tq_ref[...] = terms[:BLOCK] + terms[BLOCK:]

    def send_block(i):
        pltpu.make_async_copy(y_ref.at[i, pl.ds(0, 2)], y_hbm.at[i, pl.ds(0, 2)], row_sem).start()
        pltpu.make_async_copy(lse_ref.at[i], lse_hbm.at[i], lse_sem).start()

    send_block(g0)
    send_block(g1)

    def step(n, carry):
        blocks = sparse_blocks(n, GROUP, global_ref)
        us = range(GROUP)
        slots = [split_slots(i, width_ref, global_ref, random_ref, block_count) for i in blocks]
        k_slots = [jnp.concatenate([ks_ref[t] for t in slots[u][0]], 0) for u in us]
        v_slots = [jnp.concatenate([v_ref[t] for t in slots[u][0]], 0) for u in us]
        k_global = pair(ks_ref, g0, g1)
        v_global = pair(v_ref, g0, g1)

        def rows_of(stacked, u):
            return stacked[u * BLOCK : (u + 1) * BLOCK]

        q_raw = [q_ref[i].astype(F32) for i in blocks]
        q_scaled = [(q * gain_q).astype(BF16) for q in q_raw]
        q_all = jnp.concatenate(q_scaled, 0)
        d_out = [d_ref[i] for i in blocks]
        scores = [dot_nt(q_scaled[u], k_slots[u]) for u in us]
        scores_global = dot_nt(q_all, k_global)
        dps = [dot_nt(d_out[u], v_slots[u]) for u in us]
        dps_global = dot_nt(jnp.concatenate(d_out, 0), v_global)

        def tiles(own, shared, u):
            own_tiles = [slot_of(own[u], t) for t in range(own[u].shape[1] // BLOCK)]
            return own_tiles + [slot_of(rows_of(shared, u), t) for t in range(2)]

        s_tiles = [tiles(scores, scores_global, u) for u in us]
        d_tiles = [tiles(dps, dps_global, u) for u in us]
        tops = [
            jnp.max(functools.reduce(jnp.maximum, s_tiles[u]), axis=1, keepdims=True) * SCALE_LOG2
            for u in us
        ]
        es = [
            [
                jnp.exp2(tile * SCALE_LOG2 - (tops[u] + penalty))
                for tile, penalty in zip(s_tiles[u], slots[u][1] + slots[u][2])
            ]
            for u in us
        ]
        totals = [row_sum(functools.reduce(jnp.add, es[u])) for u in us]
        inverses = [1.0 / totals[u] for u in us]
        ps = [[e * inverses[u] for e in es[u]] for u in us]
        p_b = [[p.astype(BF16) for p in ps[u]] for u in us]
        out_global = dot_nn(
            jnp.concatenate([jnp.concatenate(p_b[u][-2:], 1) for u in us], 0), v_global
        )
        outs = [
            (dot_nn(jnp.concatenate(p_b[u][:-2], 1), v_slots[u]) + rows_of(out_global, u)).astype(BF16)
            for u in us
        ]
        row_dots = [row_sum(d_out[u].astype(F32) * outs[u].astype(F32)) for u in us]
        ds = [
            [(p * (tile - row_dots[u])).astype(BF16) for p, tile in zip(ps[u], d_tiles[u])]
            for u in us
        ]
        ds_own = [jnp.concatenate(ds[u][:-2], 1) for u in us]
        ds_global = jnp.concatenate([jnp.concatenate(ds[u][-2:], 1) for u in us], 0)
        dq_global = dot_nn(ds_global, k_global)
        dqs = [(dot_nn(ds_own[u], k_slots[u]) + rows_of(dq_global, u)) * SCALE for u in us]
        dk_t = [dot_tn(q_scaled[u], ds_own[u]) for u in us]
        dk_global = dot_tn(q_all, ds_global)
        for u in us:
            y_ref[blocks[u], 0] = outs[u]
            y_ref[blocks[u], 1] = (dqs[u] * gain_q).astype(BF16)
            lse_ref[blocks[u]] = jnp.broadcast_to(
                tops[u] + jnp.log(totals[u]) * LOG2E, (BLOCK, BLOCK)
            )
            send_block(blocks[u])
        tq_ref[...] += functools.reduce(jnp.add, [dqs[u] * q_raw[u] for u in us])
        for u in us:
            for t, block_id in enumerate(slots[u][0]):
                dk_ref[block_id] += slot_of(dk_t[u], t)
        dk_ref[g0] += slot_of(dk_global, 0)
        dk_ref[g1] += slot_of(dk_global, 1)
        return carry

    lax.fori_loop(0, (block_count - 2) // GROUP, step, 0)

    def finish(j, acc):
        dk = dk_ref[j].T * SCALE
        y_ref[j, 2] = (dk * gain_k).astype(BF16)
        return acc + dk * k_raw[j].astype(F32)

    tk = jnp.zeros((BLOCK, HD), F32)
    size = block_count // PARTS
    out_copies = []
    for part in range(PARTS):
        tk = lax.fori_loop(part * size, (part + 1) * size, finish, tk, unroll=True)
        rows = pl.ds(part * size, size)
        src, dst = y_ref.at[rows, 2], y_hbm.at[rows, 2]
        out_copies.append(pltpu.make_async_copy(src, dst, out_sems.at[part]))
        out_copies[-1].start()
    terms_ref[0:1, :] = jnp.sum(tq_ref[...], axis=0, keepdims=True)
    terms_ref[1:2, :] = jnp.sum(tk, axis=0, keepdims=True)
    for copy in out_copies:
        copy.wait()
    first = pl.ds(0, 2)
    pltpu.make_async_copy(y_ref.at[:, first], y_hbm.at[:, first], row_sem).wait()
    pltpu.make_async_copy(lse_ref, lse_hbm, lse_sem).wait()


def values_kernel(
    width_ref, global_ref, random_ref, x_hbm, gain_ref, lse_hbm, y_hbm,
    x_ref, ks_ref, lse_ref, dv_ref, y_ref, in_sems, lse_sem, out_sem,
):
    lse_copy = pltpu.make_async_copy(lse_hbm, lse_ref, lse_sem)
    lse_copy.start()
    copies = [
        pltpu.make_async_copy(x_hbm.at[:, n], x_ref.at[n], in_sems.at[n])
        for n in (KEY, QUERY, D_OUT)
    ]
    for copy in copies:
        copy.start()
    block_count = ks_ref.shape[0]
    chunks = block_count // CHUNK
    gain_q = gain_ref[0:1, :]
    g0 = global_ref[0, 0]
    g1 = global_ref[0, 1]
    q_ref, d_ref = x_ref.at[QUERY], x_ref.at[D_OUT]
    lse_copy.wait()
    for copy in copies:
        copy.wait()
    scale_keys(x_ref, ks_ref, gain_ref[1:2, :])
    q_scaled = (pair(q_ref, g0, g1).astype(F32) * gain_q).astype(BF16)
    lse = jnp.concatenate([pair(lse_ref, g0, g1)] * CHUNK, 1)
    d_out = pair(d_ref, g0, g1)

    def full_values(c, carry):
        scores = dot_nt(q_scaled, chunk_of(ks_ref, c))
        dv_t = dot_tn(d_out, jnp.exp2(scores * SCALE_LOG2 - lse).astype(BF16))
        for n in range(CHUNK):
            dv_ref[c * CHUNK + n] = slot_of(dv_t, n)
        return carry

    loop(chunks, full_values, 0)

    def step(n, carry):
        blocks = sparse_blocks(n, GROUP, global_ref)
        us = range(GROUP)
        slots = [key_slots(i, width_ref, global_ref, random_ref, block_count) for i in blocks]
        k_slots = [jnp.concatenate([ks_ref[t] for t in slots[u][0]], 0) for u in us]
        q_scaled = [(q_ref[i].astype(F32) * gain_q).astype(BF16) for i in blocks]
        scores = [dot_nt(q_scaled[u], k_slots[u]) for u in us]
        dv_t = []
        for u in us:
            lse = lse_ref[blocks[u]]
            p_b = [
                jnp.exp2(slot_of(scores[u], t) * SCALE_LOG2 - (lse + penalty)).astype(BF16)
                for t, penalty in enumerate(slots[u][1])
            ]
            dv_t.append(dot_tn(d_ref[blocks[u]], jnp.concatenate(p_b, 1)))
        for u in us:
            for t, block_id in enumerate(slots[u][0]):
                dv_ref[block_id] += slot_of(dv_t[u], t)
        return carry

    lax.fori_loop(0, (block_count - 2) // GROUP, step, 0)

    def finish(j, carry):
        y_ref[j] = dv_ref[j].T.astype(BF16)
        return carry

    loop(block_count, finish, 0, 8)
    copy = pltpu.make_async_copy(y_ref, y_hbm.at[:, pl.ds(0, BLOCK)], out_sem)
    copy.start()
    copy.wait()


def attend_without_values(widths, global_ids, random_ids, x, gains):
    blocks = x.shape[0]
    return pl.pallas_call(
        main_kernel,
        out_shape=(
            pltpu.HBM((blocks, 3, BLOCK, HD), BF16),
            pltpu.HBM((blocks, BLOCK, BLOCK), F32),
            jax.ShapeDtypeStruct((2, HD), F32),
        ),
        in_specs=[SMEM, SMEM, SMEM, HBM, VMEM],
        out_specs=(HBM, HBM, VMEM),
        scratch_shapes=[
            pltpu.VMEM((4, blocks, BLOCK, HD), BF16),
            pltpu.VMEM((blocks, BLOCK, HD), BF16),
            pltpu.VMEM((blocks // CHUNK, 2 * BLOCK, CHUNK * BLOCK), F32),
            pltpu.VMEM((blocks, HD, BLOCK), F32),
            pltpu.VMEM((blocks, 3, BLOCK, HD), BF16),
            pltpu.VMEM((blocks, BLOCK, BLOCK), F32),
            pltpu.VMEM((BLOCK, HD), F32),
            pltpu.SemaphoreType.DMA((4,)),
            pltpu.SemaphoreType.DMA((PARTS,)),
            pltpu.SemaphoreType.DMA,
            pltpu.SemaphoreType.DMA,
        ],
        compiler_params=pltpu.CompilerParams(vmem_limit_bytes=40 * MIB),
        name="attend_without_values",
    )(widths, global_ids, random_ids, *in_hbm(x), gains)


def value_gradients(widths, global_ids, random_ids, x, gains, lse):
    blocks = x.shape[0]
    return pl.pallas_call(
        values_kernel,
        out_shape=pltpu.HBM((blocks, BLOCK + TERM_ROWS, HD), BF16),
        in_specs=[SMEM, SMEM, SMEM, HBM, VMEM, HBM],
        out_specs=HBM,
        scratch_shapes=[
            pltpu.VMEM((4, blocks, BLOCK, HD), BF16),
            pltpu.VMEM((blocks, BLOCK, HD), BF16),
            pltpu.VMEM((blocks, BLOCK, BLOCK), F32),
            pltpu.VMEM((blocks, HD, BLOCK), F32),
            pltpu.VMEM((blocks, BLOCK, HD), BF16),
            pltpu.SemaphoreType.DMA((4,)),
            pltpu.SemaphoreType.DMA,
            pltpu.SemaphoreType.DMA,
        ],
        compiler_params=pltpu.CompilerParams(vmem_limit_bytes=62 * MIB),
        name="value_gradients",
    )(widths, global_ids, random_ids, *in_hbm(x), gains, *in_hbm(lse))


def put_terms_kernel(y_in, total_ref, y_out, rows_ref, sem):
    total = total_ref[...]
    high = total.astype(BF16)
    low = (total - high.astype(F32)).astype(BF16)
    rows = jnp.concatenate([high, low, jnp.zeros((TERM_ROWS - 4, HD), BF16)], 0)
    rows_ref[...] = jnp.broadcast_to(rows[None], rows_ref.shape)
    copy = pltpu.make_async_copy(rows_ref, y_out.at[:, pl.ds(BLOCK, TERM_ROWS)], sem)
    copy.start()
    copy.wait()


def put_terms(y, total):
    return pl.pallas_call(
        put_terms_kernel,
        out_shape=pltpu.HBM(y.shape, y.dtype),
        in_specs=[HBM, VMEM],
        out_specs=HBM,
        scratch_shapes=[
            pltpu.VMEM((y.shape[0], TERM_ROWS, HD), BF16),
            pltpu.SemaphoreType.DMA,
        ],
        input_output_aliases={0: 0},
        name="put_terms",
    )(*in_hbm(y), total)


def split_kernel(q_hbm, k_hbm, v_hbm, d_hbm, x_hbm, in_ref, x_ref, in_sems, out_sems):
    sources = (q_hbm, k_hbm, v_hbm, d_hbm)
    heads = x_ref.shape[0] // PARTS
    width = heads * HD

    def fetch(c, n):
        src = sources[n].at[0, :, pl.ds(c * width, width)]
        return pltpu.make_async_copy(src, in_ref.at[c, n], in_sems.at[c, n])

    def send(c):
        part = pl.ds(c * heads, heads)
        return pltpu.make_async_copy(x_ref.at[part], x_hbm.at[part], out_sems.at[c])

    for c in range(PARTS):
        for n in range(4):
            fetch(c, n).start()
    for c in range(PARTS):
        for n in range(4):
            fetch(c, n).wait()
            for h in range(heads):
                x_ref[c * heads + h, n] = in_ref[c, n, :, h * HD : (h + 1) * HD]
        send(c).start()
    for c in range(PARTS):
        send(c).wait()


def split_heads(arrays):
    _, tokens, channels = arrays[0].shape
    heads = channels // HD
    return pl.pallas_call(
        split_kernel,
        out_shape=pltpu.HBM((heads, 4, tokens, HD), BF16),
        in_specs=[HBM] * 4,
        out_specs=HBM,
        scratch_shapes=[
            pltpu.VMEM((PARTS, 4, tokens, channels // PARTS), BF16),
            pltpu.VMEM((heads, 4, tokens, HD), BF16),
            pltpu.SemaphoreType.DMA((PARTS, 4)),
            pltpu.SemaphoreType.DMA((PARTS,)),
        ],
        compiler_params=pltpu.CompilerParams(vmem_limit_bytes=16 * MIB),
        name="split_heads",
    )(*in_hbm(*arrays))


def join_kernel(z_hbm, a_hbm, b_hbm, c_hbm, in_ref, out_ref, in_sems, out_sems):
    targets = (a_hbm, b_hbm, c_hbm)
    heads = in_ref.shape[0] // PARTS
    width = heads * HD

    def fetch(c):
        part = pl.ds(c * heads, heads)
        return pltpu.make_async_copy(z_hbm.at[part], in_ref.at[part], in_sems.at[c])

    def send(c, n):
        dst = targets[n].at[0, :, pl.ds(c * width, width)]
        return pltpu.make_async_copy(out_ref.at[c, n], dst, out_sems.at[c, n])

    for c in range(PARTS):
        fetch(c).start()
    for c in range(PARTS):
        fetch(c).wait()
        for n in range(3):
            for h in range(heads):
                out_ref[c, n, :, h * HD : (h + 1) * HD] = in_ref[c * heads + h, n]
            send(c, n).start()
    for c in range(PARTS):
        for n in range(3):
            send(c, n).wait()


def join_terms_kernel(place_ref, z_ref, a_hbm, gains_ref, out_ref, out_sems):
    heads = z_ref.shape[0] // PARTS
    width = heads * HD
    copies = []
    for c in range(PARTS):
        for h in range(heads):
            out_ref[c, :, h * HD : (h + 1) * HD] = z_ref[c * heads + h, 0:BLOCK]
        dst = a_hbm.at[0, :, pl.ds(c * width, width)]
        copies.append(pltpu.make_async_copy(out_ref.at[c], dst, out_sems.at[c]))
        copies[-1].start()
    own = gains_ref.shape[1] // HD
    for n in range(own):
        rows = z_ref[place_ref[0] * own + n, BLOCK : BLOCK + TERM_ROWS].astype(F32)
        gains_ref[:, n * HD : (n + 1) * HD] = rows[0:2] + rows[2:4]
    for copy in copies:
        copy.wait()


def join_heads(z):
    heads = z.shape[0]
    return pl.pallas_call(
        join_kernel,
        out_shape=(pltpu.HBM((1, BLOCK, heads * HD), BF16),) * 3,
        in_specs=[HBM],
        out_specs=(HBM,) * 3,
        scratch_shapes=[
            pltpu.VMEM((heads, 3, BLOCK, HD), BF16),
            pltpu.VMEM((PARTS, 3, BLOCK, heads * HD // PARTS), BF16),
            pltpu.SemaphoreType.DMA((PARTS,)),
            pltpu.SemaphoreType.DMA((PARTS, 3)),
        ],
        compiler_params=pltpu.CompilerParams(vmem_limit_bytes=16 * MIB),
        name="join_heads",
    )(*in_hbm(z))


def join_heads_terms(place, z, own):
    heads = z.shape[0]
    return pl.pallas_call(
        join_terms_kernel,
        out_shape=(
            pltpu.HBM((1, BLOCK, heads * HD), BF16),
            jax.ShapeDtypeStruct((2, own * HD), F32),
        ),
        in_specs=[SMEM, VMEM],
        out_specs=(HBM, VMEM),
        scratch_shapes=[
            pltpu.VMEM((PARTS, BLOCK, heads * HD // PARTS), BF16),
            pltpu.SemaphoreType.DMA((PARTS,)),
        ],
        compiler_params=pltpu.CompilerParams(vmem_limit_bytes=16 * MIB),
        name="join_heads_terms",
    )(place, z)


def exchange(x):
    return lax.all_to_all(x, "ctx", split_axis=0, concat_axis=0, tiled=True)


def sum_over_sequences(terms):
    count = lax.axis_size("dp")
    stride = 1
    while stride < count:
        pairs = [(n, n ^ stride) for n in range(count)]
        terms = terms + lax.ppermute(terms, "dp", pairs)
        stride *= 2
    return terms


def on_device(queries, keys, values, d_out, gains, window_widths, global_blocks, random_blocks):
    x = exchange(split_heads((queries, keys, values, d_out)))
    all_gains = lax.all_gather(gains, "dp", axis=1, tiled=True)
    own_gains = lax.dynamic_slice_in_dim(all_gains, lax.axis_index("ctx") * HD, HD, 1)
    tables = (window_widths, global_blocks, random_blocks)
    y, lse, terms = attend_without_values(*tables, x, own_gains)
    returned = exchange(y)
    d_values = value_gradients(*tables, x, own_gains, lse)
    d_values = put_terms(d_values, sum_over_sequences(terms))
    d_values, returned = lax.optimization_barrier((d_values, returned))
    out, d_queries, d_keys = join_heads(returned)
    place = lax.axis_index("dp").reshape(1)
    d_values, d_gains = join_heads_terms(place, exchange(d_values), gains.shape[1] // HD)
    return (out, d_queries, d_keys, d_values, d_gains)


def solution(mesh):
    tokens = P("dp", "ctx", None)
    return jax.shard_map(
        on_device,
        mesh=mesh,
        in_specs=(
            tokens, tokens, tokens, tokens,
            P(None, "dp"), P("ctx"), P("dp", None), P("dp", None, None),
        ),
        out_specs=(tokens, tokens, tokens, tokens, P(None, "dp")),
        check_vma=False,
    )
```
